256 devices in a mesh: grp: 4 (over z_lo), row: 4 (over x), col: 16 (over y, z_hi, core).
Axes of the slice: x: 4, y: 4, z: 8 (z_hi: 2, z_lo: 4; z = z_hi * 4 + z_lo), core: 2. Of those that a mesh axis runs over, the one named last changes fastest.
Arguments:
- outer_params: float32 [8192, 1024], P('col', 'row'), may hold values from -0.0625 to 0.0625
- first_moment: float32 [4, 8192, 1024], P('grp', 'col', 'row'), may hold values from -0.12 to 0.12
- second_moment: float32 [4, 8192, 1024], P('grp', 'col', 'row'), may hold values from 0.0001 to 0.01
- outer_moment: float32 [8192, 1024], P('col', 'row'), may hold values from -0.06 to 0.06
- activations: bfloat16 [4, 3, 2048, 8192], P('grp', None, 'row', 'col'), may hold values from -6 to 6
- targets: bfloat16 [4, 3, 2048, 1024], P('grp', None, 'col', 'row'), may hold values from -6 to 6
Outputs:
- new_params: float32 [8192, 1024], P('col', 'row')
- new_moment: float32 [8192, 1024], P('col', 'row')
The draws below stay inside these ranges and needn't reach their ends.
All inputs are finite; a program needn't handle non-finite values.
Results may differ from the reference program's by a relative error of at most 0.0054.
Values may be sent and summed in bfloat16 or wider, within the bound.
A program may use at most 64 MiB of HBM per device.

```python
import math
import jax
import jax.numpy as jnp

D = 8192
TOKENS = 2048
STEPS = 3
SLOW_STEPS = 1
PRIOR = 100
H = 1024
UNITS = 4


def block_levels(stream_key, shape, pieces, least, high):
    def one(axis_at, parts):
        heights = jax.random.uniform(jax.random.fold_in(jax.random.fold_in(stream_key, 6), axis_at), (parts,), jnp.float32, least / len(pieces), high / len(pieces))
        return jnp.repeat(jnp.exp(heights), shape[axis_at] // parts).reshape((-1,) + (1,) * (len(shape) - axis_at - 1))

    loudness = one(*pieces[0])
    for cut in pieces[1:]:
        loudness = loudness * one(*cut)
    return loudness


def noise(stream_key, shape, width, most, pieces=(), held_as=jnp.bfloat16):
    level = block_levels(stream_key, shape, pieces, -0.22, 0.18) if pieces else 1.0
    drawn = jax.random.normal(stream_key, shape, jnp.float32) * width * level
    return jnp.minimum(jnp.maximum(drawn, -most), most).astype(held_as)


def setup_inputs(seed: int = 0) -> dict:
    key_of = jax.random.split(jax.random.key(seed), 7)
    outer_params = noise(key_of[0], (D, H), D ** -0.5, 0.0625, ((0, 16), (1, 4)), jnp.float32)
    first_moment = noise(key_of[1], (UNITS, D, H), 0.02, 0.12, ((0, 4), (1, 16), (2, 4)), jnp.float32)
    second_moment = jnp.clip(jnp.exp(math.log(0.01) - 4.6051702 * jax.random.uniform(key_of[2], (UNITS, D, H), jnp.float32) ** block_levels(key_of[2], (UNITS, D, H), ((0, 4), (1, 16), (2, 4)), -0.2, 0.2)), 0.0001, 0.01)
    outer_moment = noise(key_of[3], (D, H), 0.01, 0.06, ((0, 16), (1, 4)), jnp.float32)
    activations = noise(key_of[4], (UNITS, STEPS, TOKENS, D), 1.0, 6.0, ((0, 4), (2, 4), (3, 16)))
    targets = noise(key_of[5], (UNITS, STEPS, TOKENS, H), 1.0, 6.0, ((0, 4), (2, 16), (3, 4)))
    return {"outer_params": outer_params, "first_moment": first_moment, "second_moment": second_moment, "outer_moment": outer_moment, "activations": activations, "targets": targets}


beta_first = 0.9
beta_second = 0.95
inner_rate = 0.01
decay_rate = 0.1
epsilon_value = 1e-08
outer_rate = 0.7
momentum_coef = 0.9

def inner_steps(params, first, second, inputs, wanted, count):
    for inner_step in range(count):
        output = jnp.dot(inputs[inner_step], params.astype(jnp.bfloat16), preferred_element_type=jnp.float32)
        residual = (output - wanted[inner_step].astype(jnp.float32)).astype(jnp.bfloat16)
        gradient = jnp.dot(inputs[inner_step].T, residual, preferred_element_type=jnp.float32) / TOKENS
        first = beta_first * first + (1.0 - beta_first) * gradient
        second = beta_second * second + (1.0 - beta_second) * gradient * gradient
        power = PRIOR + inner_step + 1
        corrected = first / (1.0 - beta_first ** power) / (jnp.sqrt(second / (1.0 - beta_second ** power)) + epsilon_value)
        params = params - inner_rate * (corrected + decay_rate * params)
    return params

def reference(outer_params, first_moment, second_moment, outer_moment, activations, targets):
    total_steps = 3 * STEPS + SLOW_STEPS
    pseudo = jnp.zeros(outer_params.shape, jnp.float32)
    for unit_index in range(4):
        count = STEPS if unit_index < 3 else SLOW_STEPS
        local = inner_steps(outer_params, first_moment[unit_index], second_moment[unit_index], activations[unit_index], targets[unit_index], count)
        pseudo = pseudo + float(count) / float(total_steps) * (outer_params - local)
    new_moment = momentum_coef * outer_moment + pseudo
    new_params = outer_params - outer_rate * (pseudo + momentum_coef * new_moment)
    return (new_params, new_moment)
```

```python
import functools

import jax
import jax.numpy as jnp
from jax import lax
from jax.experimental import pallas as pl
from jax.experimental.pallas import tpu as pltpu
from jax.sharding import PartitionSpec as P

TOKENS = 2048
STEPS = 3
SLOW_STEPS = 1
PRIOR = 100
BLOCK = 512
PART = 128

beta_first = 0.9
beta_second = 0.95
inner_rate = 0.01
decay_rate = 0.1
epsilon_value = 1e-08
outer_rate = 0.7
momentum_coef = 0.9

F32 = jnp.float32
BF16 = jnp.bfloat16


def dot_nt(a, b):
    return lax.dot_general(a, b, (((1,), (1,)), ((), ())), preferred_element_type=F32)


def dot_nn(a, b):
    return lax.dot_general(a, b, (((1,), (0,)), ((), ())), preferred_element_type=F32)


def kernel(
    w_in, m_in, v_in, x_in, t_in, o_ref,
    xg, raw, wt, mt, vt, ot, wb, traw, own, ysend, yrecv, ysum, zsend, zrecv, resid, grad,
    dsend, drecv, pall, back, stage,
    lsem, xs, xr, ss, sr, ws, wr, ts, tr, ys, yr, zs, zr, gs, gr, ds_, dr, ps, pr, bs, br,
):
    g = lax.axis_index("grp")
    x = lax.axis_index("row")
    col = lax.axis_index("col")
    y = col // 4
    zh = (col // 2) % 2
    k = col % 2

    sib = {"col": col + 1 - 2 * k}
    zdev = {"col": y * 4 + (1 - zh) * 2 + k}
    right = {"row": (x + 1) % 4}
    left = {"row": (x + 3) % 4}
    xl, xr_, xo = (x + 3) % 4, (x + 1) % 4, (x + 2) % 4

    def ydev(j):
        return {"col": ((y + j) % 4) * 4 + zh * 2 + k}

    def gdev(j):
        return {"grp": (g + j) % 4}

    def quad(n):
        c = (zh * 2 + k + n) % 4
        return c, {"col": y * 4 + c}

    def remote(src, dst, s_sem, r_sem, dev):
        return pltpu.make_async_remote_copy(
            src_ref=src, dst_ref=dst, send_sem=s_sem, recv_sem=r_sem,
            device_id=dev, device_id_type=pl.DeviceIdType.MESH,
        )

    barrier = pltpu.get_barrier_semaphore()
    peers = [sib, right, left] + [ydev(j) for j in (1, 2, 3)]
    peers += [gdev(j) for j in (1, 2, 3)] + [quad(n)[1] for n in (1, 2, 3)]
    for dev in peers:
        pl.semaphore_signal(barrier, inc=1, device_id=dev, device_id_type=pl.DeviceIdType.MESH)

    mine = pl.ds(pl.multiple_of(k * PART, PART), PART)
    other = pl.ds(pl.multiple_of((1 - k) * PART, PART), PART)
    locals_ = [pltpu.make_async_copy(w_in.at[:, mine], raw.at[0, k], lsem.at[0])]
    locals_ += [pltpu.make_async_copy(x_in.at[0, s], xg.at[s, x, k], lsem.at[1 + s]) for s in range(STEPS)]
    locals_ += [pltpu.make_async_copy(m_in.at[0, :, mine], raw.at[1, k], lsem.at[4])]
    locals_ += [pltpu.make_async_copy(v_in.at[0, :, mine], raw.at[2, k], lsem.at[5])]
    me4 = zh * 2 + k
    locals_ += [pltpu.make_async_copy(t_in.at[0, :, :, mine], traw.at[me4], lsem.at[6])]
    for c in locals_:
        c.start()

    pl.semaphore_wait(barrier, len(peers))

    halves = (pl.ds(0, 256), pl.ds(256, 256))

    def x_own(s, h, way):
        return remote(
            x_in.at[0, s, halves[h]], xg.at[s, x, k, halves[h]],
            xs.at[s, 2 * way + h], xr.at[s, 2 * way + h], (right, left)[way],
        )

    def x_from(s, h, way):
        src = (xl, xr_)[way]
        return remote(
            xg.at[s, src, k, halves[h]], xg.at[s, src, k, halves[h]],
            xs.at[s, 2 * way + h], xr.at[s, 2 * way + h], (right, left)[way],
        )

    def x_fwd(s, way):
        src = (xl, xr_)[way]
        return remote(
            xg.at[s, src, k, halves[way]], xg.at[s, src, k, halves[way]],
            xs.at[s, 4 + way], xr.at[s, 4 + way], (right, left)[way],
        )

    def x_opp(s, way):
        return remote(
            xg.at[s, xo, k, halves[way]], xg.at[s, xo, k, halves[way]],
            xs.at[s, 4 + way], xr.at[s, 4 + way], (right, left)[way],
        )

    def x_sib(s, d, h, src=None):
        b = (x + d) % 4
        return remote(
            xg.at[s, b, k, halves[h]] if src is None else src, xg.at[s, b, k, halves[h]],
            ss.at[s, 2 * d + h], sr.at[s, 2 * d + h], sib,
        )

    def x_sib_in(s, d, h):
        b = (x + d) % 4
        return remote(
            xg.at[s, b, 1 - k, halves[h]], xg.at[s, b, 1 - k, halves[h]],
            ss.at[s, 2 * d + h], sr.at[s, 2 * d + h], sib,
        )

    def x_begin(s):
        x_own(s, 0, 0).start()
        x_own(s, 1, 1).start()
        x_own(s, 1, 0).start()
        x_own(s, 0, 1).start()
        for h in range(2):
            x_sib(s, 0, h, x_in.at[0, s, halves[h]]).start()

    def x_middle(s):
        x_from(s, 0, 0).wait_recv()
        x_fwd(s, 0).start()
        x_sib(s, 3, 0).start()
        x_from(s, 1, 1).wait_recv()
        x_fwd(s, 1).start()
        x_sib(s, 1, 1).start()
        x_from(s, 1, 0).wait_recv()
        x_sib(s, 3, 1).start()
        x_from(s, 0, 1).wait_recv()
        x_sib(s, 1, 0).start()

    def x_end(s):
        for way in range(2):
            x_opp(s, way).wait_recv()
            x_sib(s, 2, way).start()

    def swap(i, ref):
        return remote(ref, raw.at[i, k], ws.at[i], wr.at[i], sib)

    def swap_in(i):
        return remote(raw.at[i, 1 - k], raw.at[i, 1 - k], ws.at[i], wr.at[i], sib)

    def t_out(n):
        c, dev = quad(n)
        half = pl.ds(pl.multiple_of((c % 2) * PART, PART), PART)
        return remote(t_in.at[0, :, :, half], traw.at[me4], ts.at[n], tr.at[n], dev)

    def t_from(n):
        c, dev = quad(4 - n)
        return remote(traw.at[c], traw.at[c], ts.at[n], tr.at[n], dev)

    swap(0, w_in.at[:, other]).start()
    x_begin(0)
    swap(1, m_in.at[0, :, other]).start()
    swap(2, v_in.at[0, :, other]).start()
    for n in (1, 2, 3):
        t_out(n).start()

    def turned(i, dst):
        for kd in range(2):
            for r in range(4):
                dst[:, kd * BLOCK + r * PART : kd * BLOCK + (r + 1) * PART] = raw[
                    i, kd, r * PART : (r + 1) * PART, :
                ].T

    locals_[0].wait()
    swap_in(0).wait_recv()
    turned(0, wt)
    ot[...] = wt[...]
    wb[...] = wt[...].astype(BF16)
    locals_[4].wait()
    locals_[5].wait()
    swap_in(1).wait_recv()
    turned(1, mt)
    swap_in(2).wait_recv()
    turned(2, vt)

    def partial_of(s, b, q):
        rows = pl.ds(q * PART, PART)
        return dot_nt(wb[:, :BLOCK], xg[s, b, 0, rows, :]) + dot_nt(wb[:, BLOCK:], xg[s, b, 1, rows, :])

    def y_out(s, j, q):
        return remote(ysend.at[s, j, q], yrecv.at[s, j, q], ys.at[s, j, q], yr.at[s, j, q], ydev(j))

    def z_out(s, q):
        return remote(zsend.at[s, q], zrecv.at[s, q], zs.at[s, q], zr.at[s, q], zdev)

    def g_out(s, j, q):
        return remote(resid.at[s, y, q], resid.at[s, y, q], gs.at[s, j, q], gr.at[s, j, q], ydev(j))

    def g_from(s, j, q):
        b = (y + 4 - j) % 4
        return remote(resid.at[s, b, q], resid.at[s, b, q], gs.at[s, j, q], gr.at[s, j, q], ydev(j))

    def forward_block(s, b):
        j = (b + 4 - y) % 4
        for q in range(4):
            value = partial_of(s, b, q)

            @pl.when(j == 0)
            def _():
                own[q] = value

            @pl.when(j != 0)
            def _():
                ysend[s, j, q] = value.astype(BF16)
                y_out(s, j, q).start()

    def forward_pieces(s):
        for q in range(4):
            for j in (2, 1, 3):
                ysend[s, j, q] = partial_of(s, (y + j) % 4, q).astype(BF16)
                y_out(s, j, q).start()
            own[q] = partial_of(s, y, q)

    def middle(s):
        for q in range(4):
            total = own[q]
            for j in (1, 3, 2):
                y_out(s, j, q).wait_recv()
                total = total + yrecv[s, j, q].astype(F32)
            ysum[q] = total
            zsend[s, q] = total.astype(BF16)
            z_out(s, q).start()
        for q in range(4):
            wanted = traw[q, s].astype(F32).T
            z_out(s, q).wait_recv()
            output = ysum[q] + zrecv[s, q].astype(F32)
            resid[s, y, q] = (output - wanted).astype(BF16)
            for j in (2, 1, 3):
                g_out(s, j, q).start()

    def backward(s):
        r = jnp.concatenate([resid[s, y, q] for q in range(4)], axis=1)
        for kd in range(2):
            grad[:, kd * BLOCK : (kd + 1) * BLOCK] = dot_nn(r, xg[s, y, kd])
        for h in range(2):
            for j in (1, 3, 2):
                b = (y + 4 - j) % 4
                for q in (2 * h, 2 * h + 1):
                    g_from(s, j, q).wait_recv()
                r = jnp.concatenate([resid[s, b, 2 * h], resid[s, b, 2 * h + 1]], axis=1)
                for kd in range(2):
                    grad[:, kd * BLOCK : (kd + 1) * BLOCK] += dot_nn(r, xg[s, b, kd, halves[h], :])

    def update(s):
        power = PRIOR + s + 1

        @pl.loop(0, PART // 16)
        def _(i):
            rows = pl.ds(pl.multiple_of(i * 16, 16), 16)
            for cut in range(2):
                at = (rows, slice(cut * BLOCK, (cut + 1) * BLOCK))
                gradient = grad[at] * (1.0 / TOKENS)
                first = beta_first * mt[at] + (1.0 - beta_first) * gradient
                second = beta_second * vt[at] + (1.0 - beta_second) * gradient * gradient
                corrected = (
                    first
                    / (1.0 - beta_first**power)
                    / (jnp.sqrt(second / (1.0 - beta_second**power)) + epsilon_value)
                )
                old = wt[at]
                new = old - inner_rate * (corrected + decay_rate * old)
                mt[at] = first
                vt[at] = second
                wt[at] = new
                if s + 1 < STEPS:
                    wb[at] = new.astype(BF16)

    def x_arrived(s, d):
        for h in range(2):
            x_sib_in(s, d, h).wait_recv()

    locals_[1].wait()
    x_arrived(0, 0)
    forward_block(0, x)
    x_middle(0)
    x_arrived(0, 3)
    forward_block(0, xl)
    x_arrived(0, 1)
    forward_block(0, xr_)
    x_end(0)

    fast = g < 3

    @pl.when(fast)
    def _():
        x_begin(1)

    x_arrived(0, 2)
    forward_block(0, xo)
    locals_[6].wait()
    for n in (1, 2, 3):
        t_from(n).wait_recv()
    middle(0)

    @pl.when(fast)
    def _():
        x_middle(1)

    backward(0)
    update(0)

    locals_[2].wait()
    locals_[3].wait()

    @pl.when(fast)
    def _():
        for s in range(1, STEPS):
            x_end(s)
            if s + 1 < STEPS:
                x_begin(s + 1)
            for d in (0, 3, 1, 2):
                x_arrived(s, d)
            forward_pieces(s)
            middle(s)
            if s + 1 < STEPS:
                x_middle(s + 1)
            backward(s)
            update(s)

    weight = jnp.where(fast, float(STEPS), float(SLOW_STEPS)) / float(3 * STEPS + SLOW_STEPS)
    for i in range(4):
        cols = pl.ds(i * 256, 256)
        dsend[i] = weight * (ot[:, cols] - wt[:, cols])

    def d_out(j):
        return remote(dsend.at[(g + j) % 4], drecv.at[j], ds_.at[j], dr.at[j], gdev(j))

    def p_out(j):
        return remote(pall.at[g], pall.at[g], ps.at[j], pr.at[j], gdev(j))

    def p_from(j):
        c = (g + 4 - j) % 4
        return remote(pall.at[c], pall.at[c], ps.at[j], pr.at[j], gdev(j))

    for j in (2, 1, 3):
        d_out(j).start()
    total = dsend[g]
    for j in (1, 3, 2):
        d_out(j).wait_recv()
        total = total + drecv[j]
    pall[g] = total
    for j in (2, 1, 3):
        p_out(j).start()
    for j in (1, 3, 2):
        p_from(j).wait_recv()

    for i in range(4):
        for r in range(2):
            rows = slice((i % 2) * 256 + r * PART, (i % 2) * 256 + (r + 1) * PART)
            stage[i // 2, rows, :] = pall[i, :, r * PART : (r + 1) * PART].T
    away = remote(stage.at[1 - k], back, bs, br, sib)
    away.start()
    away.wait_recv()

    @pl.when(k == 0)
    def _():
        o_ref[:, :PART] = stage[0]
        o_ref[:, PART:] = back[...]

    @pl.when(k == 1)
    def _():
        o_ref[:, :PART] = back[...]
        o_ref[:, PART:] = stage[1]

    away.wait_send()
    for j in (1, 2, 3):
        d_out(j).wait_send()
        p_out(j).wait_send()
    for i in range(3):
        swap_in(i).wait_send()
    for n in (1, 2, 3):
        t_from(n).wait_send()

    def sent(s):
        for way in range(2):
            for h in range(2):
                x_own(s, h, way).wait_send()
            x_fwd(s, way).wait_send()
        for d in range(4):
            for h in range(2):
                x_sib(s, d, h).wait_send()
        for q in range(4):
            for j in (1, 2, 3):
                y_out(s, j, q).wait_send()
                g_out(s, j, q).wait_send()
            z_out(s, q).wait_send()

    sent(0)

    @pl.when(fast)
    def _():
        for s in range(1, STEPS):
            sent(s)


def pseudo_of(outer_params, first_moment, second_moment, activations, targets):
    dma = pltpu.SemaphoreType.DMA
    vm = pltpu.VMEM
    any_ = pl.BlockSpec(memory_space=pl.ANY)
    n = STEPS
    return pl.pallas_call(
        kernel,
        out_shape=jax.ShapeDtypeStruct((512, 256), F32),
        in_specs=[any_] * 5,
        out_specs=pl.BlockSpec(memory_space=pltpu.VMEM),
        scratch_shapes=[
            vm((n, 4, 2, 512, 512), BF16),
            vm((3, 2, 512, PART), F32),
            vm((PART, 1024), F32), vm((PART, 1024), F32), vm((PART, 1024), F32), vm((PART, 1024), F32),
            vm((PART, 1024), BF16),
            vm((4, n, PART, PART), BF16),
            vm((4, PART, PART), F32),
            vm((n, 4, 4, PART, PART), BF16), vm((n, 4, 4, PART, PART), BF16),
            vm((4, PART, PART), F32),
            vm((n, 4, PART, PART), BF16), vm((n, 4, PART, PART), BF16),
            vm((n, 4, 4, PART, PART), BF16),
            vm((PART, 1024), F32),
            vm((4, PART, 256), F32), vm((4, PART, 256), F32), vm((4, PART, 256), F32),
            vm((512, PART), F32),
            vm((2, 512, PART), F32),
            dma((7,)),
            dma((n, 6)), dma((n, 6)), dma((n, 8)), dma((n, 8)),
            dma((3,)), dma((3,)), dma((4,)), dma((4,)),
            dma((n, 4, 4)), dma((n, 4, 4)), dma((n, 4)), dma((n, 4)),
            dma((n, 4, 4)), dma((n, 4, 4)), dma((4,)), dma((4,)), dma((4,)), dma((4,)),
            dma, dma,
        ],
        compiler_params=pltpu.CompilerParams(
            collective_id=0, has_side_effects=True, vmem_limit_bytes=48 << 20
        ),
    )(outer_params, first_moment, second_moment, activations, targets)


def local(outer_params, first_moment, second_moment, outer_moment, activations, targets):
    pseudo = pseudo_of(outer_params, first_moment, second_moment, activations, targets)
    new_moment = momentum_coef * outer_moment + pseudo
    new_params = outer_params - outer_rate * (pseudo + momentum_coef * new_moment)
    return (new_params, new_moment)


def solution(mesh):
    placed = (
        P("col", "row"),
        P("grp", "col", "row"),
        P("grp", "col", "row"),
        P("col", "row"),
        P("grp", None, "row", "col"),
        P("grp", None, "col", "row"),
    )
    return jax.shard_map(
        local,
        mesh=mesh,
        in_specs=placed,
        out_specs=(P("col", "row"), P("col", "row")),
        check_vma=False,
    )
```

```python
import functools

import jax
import jax.numpy as jnp
from jax import lax
from jax.experimental import pallas as pl
from jax.experimental.pallas import tpu as pltpu
from jax.sharding import PartitionSpec as P

TOKENS = 2048
STEPS = 3
SLOW_STEPS = 1
PRIOR = 100
BLOCK = 512
PART = 128

beta_first = 0.9
beta_second = 0.95
inner_rate = 0.01
decay_rate = 0.1
epsilon_value = 1e-08
outer_rate = 0.7
momentum_coef = 0.9

F32 = jnp.float32
BF16 = jnp.bfloat16


def dot_nt(a, b):
    return lax.dot_general(a, b, (((1,), (1,)), ((), ())), preferred_element_type=F32)


def dot_nn(a, b):
    return lax.dot_general(a, b, (((1,), (0,)), ((), ())), preferred_element_type=F32)


def kernel(
    w_in, m_in, v_in, x_in, t_in, o_ref,
    xg, raw, wt, mt, vt, ot, wb, traw, own, ysend, yrecv, ysum, zsend, zrecv, resid, grad,
    slow, slow_in, early, early_in, early_sum, left_over, late, late_in, late_sum, stage, back,
    lsem, xs, xr, ss, sr, ws, wr, ts, tr, ys, yr, zs, zr, gs, gr,
    os_, or_, es, er, as_, ar, ls, lr, fs, fr, bs, br,
):
    g = lax.axis_index("grp")
    x = lax.axis_index("row")
    col = lax.axis_index("col")
    y = col // 4
    zh = (col // 2) % 2
    k = col % 2

    def flip(g_, y_, zh_):
        return (y_ // 2 + zh_ + g_) % 2

    role = (k + flip(g, y, zh)) % 2

    def at(g_, y_, zh_):
        return {"grp": g_, "col": y_ * 4 + zh_ * 2 + (role + flip(g_, y_, zh_)) % 2}

    sib = {"col": y * 4 + zh * 2 + (1 - k)}
    zdev = at(g, y, 1 - zh)
    across = y * 4 + zh * 2 + (1 - k)
    right = {"row": (x + 1) % 4, "col": across}
    left = {"row": (x + 3) % 4, "col": across}
    xl, xr_, xo = (x + 3) % 4, (x + 1) % 4, (x + 2) % 4

    def ydev(j):
        return at(g, (y + j) % 4, zh)

    def gdev(j):
        return at((g + j) % 4, y, zh)

    def remote(src, dst, s_sem, r_sem, dev):
        return pltpu.make_async_remote_copy(
            src_ref=src, dst_ref=dst, send_sem=s_sem, recv_sem=r_sem,
            device_id=dev, device_id_type=pl.DeviceIdType.MESH,
        )

    barrier = pltpu.get_barrier_semaphore()
    peers = [sib, right, left, zdev] + [ydev(j) for j in (1, 2, 3)] + [gdev(j) for j in (1, 2, 3)]
    for dev in peers:
        pl.semaphore_signal(barrier, inc=1, device_id=dev, device_id_type=pl.DeviceIdType.MESH)

    mine = pl.ds(pl.multiple_of(role * PART, PART), PART)
    other = pl.ds(pl.multiple_of((1 - role) * PART, PART), PART)
    locals_ = [pltpu.make_async_copy(w_in.at[:, mine], raw.at[0, k], lsem.at[0])]
    locals_ += [pltpu.make_async_copy(x_in.at[0, s], xg.at[s, x, k], lsem.at[1 + s]) for s in range(STEPS)]
    locals_ += [pltpu.make_async_copy(m_in.at[0, :, mine], raw.at[1, k], lsem.at[4])]
    locals_ += [pltpu.make_async_copy(v_in.at[0, :, mine], raw.at[2, k], lsem.at[5])]
    locals_ += [pltpu.make_async_copy(t_in.at[0, :, :, mine], traw.at[k], lsem.at[6])]
    for c in locals_:
        c.start()

    pl.semaphore_wait(barrier, len(peers))

    halves = (pl.ds(0, 256), pl.ds(256, 256))

    def x_copy(s, slot, src, dst, way):
        return remote(src, dst, xs.at[s, slot], xr.at[s, slot], (right, left)[way])

    def x_own(s, h, way):
        return x_copy(s, 2 * way + h, x_in.at[0, s, halves[h]], xg.at[s, x, k, halves[h]], way)

    def x_from(s, h, way):
        here = xg.at[s, (xl, xr_)[way], 1 - k, halves[h]]
        return x_copy(s, 2 * way + h, here, here, way)

    def x_fwd(s, way):
        here = xg.at[s, (xl, xr_)[way], 1 - k, halves[way]]
        return x_copy(s, 4 + way, here, here, way)

    def x_opp(s, way):
        here = xg.at[s, xo, k, halves[way]]
        return x_copy(s, 4 + way, here, here, way)

    def x_sib(s, d, h, src=None, incoming=False):
        kd = (k + d + incoming) % 2
        here = xg.at[s, (x + d) % 4, kd, halves[h]]
        return remote(here if src is None else src, here, ss.at[s, 2 * d + h], sr.at[s, 2 * d + h], sib)

    def x_begin(s):
        x_own(s, 0, 0).start()
        x_own(s, 1, 1).start()
        x_own(s, 1, 0).start()
        x_own(s, 0, 1).start()
        for h in range(2):
            x_sib(s, 0, h, x_in.at[0, s, halves[h]]).start()

    def x_middle(s):
        x_from(s, 0, 0).wait_recv()
        x_fwd(s, 0).start()
        x_sib(s, 3, 0).start()
        x_from(s, 1, 1).wait_recv()
        x_fwd(s, 1).start()
        x_sib(s, 1, 1).start()
        x_from(s, 1, 0).wait_recv()
        x_sib(s, 3, 1).start()
        x_from(s, 0, 1).wait_recv()
        x_sib(s, 1, 0).start()

    def x_end(s):
        for way in range(2):
            x_opp(s, way).wait_recv()
            x_sib(s, 2, way).start()

    def swap(i, ref):
        return remote(ref, raw.at[i, k], ws.at[i], wr.at[i], sib)

    def swap_in(i):
        return remote(raw.at[i, 1 - k], raw.at[i, 1 - k], ws.at[i], wr.at[i], sib)

    def t_swap(kd):
        return remote(t_in.at[0, :, :, other], traw.at[kd], ts, tr, sib)

    swap(0, w_in.at[:, other]).start()
    x_begin(0)
    swap(1, m_in.at[0, :, other]).start()
    swap(2, v_in.at[0, :, other]).start()
    t_swap(k).start()

    def turned(i, dst):
        for kd in range(2):
            for r in range(4):
                dst[:, kd * BLOCK + r * PART : kd * BLOCK + (r + 1) * PART] = raw[
                    i, kd, r * PART : (r + 1) * PART, :
                ].T

    locals_[0].wait()
    swap_in(0).wait_recv()
    turned(0, wt)
    ot[...] = wt[...]
    wb[...] = wt[...].astype(BF16)
    locals_[4].wait()
    locals_[5].wait()
    swap_in(1).wait_recv()
    turned(1, mt)
    swap_in(2).wait_recv()
    turned(2, vt)

    def partial_of(s, b, q):
        rows = pl.ds(q * PART, PART)
        return dot_nt(wb[:, :BLOCK], xg[s, b, 0, rows, :]) + dot_nt(wb[:, BLOCK:], xg[s, b, 1, rows, :])

    def y_out(s, j, q):
        return remote(ysend.at[s, j, q], yrecv.at[s, j, q], ys.at[s, j, q], yr.at[s, j, q], ydev(j))

    def z_out(s, q):
        return remote(zsend.at[s, q], zrecv.at[s, q], zs.at[s, q], zr.at[s, q], zdev)

    def g_out(s, j, q):
        return remote(resid.at[s, y, q], resid.at[s, y, q], gs.at[s, j, q], gr.at[s, j, q], ydev(j))

    def g_from(s, j, q):
        b = (y + 4 - j) % 4
        return remote(resid.at[s, b, q], resid.at[s, b, q], gs.at[s, j, q], gr.at[s, j, q], ydev(j))

    def forward_block(s, b):
        j = (b + 4 - y) % 4
        for q in range(4):
            value = partial_of(s, b, q)

            @pl.when(j == 0)
            def _():
                own[q] = value

            @pl.when(j != 0)
            def _():
                ysend[s, j, q] = value.astype(BF16)
                y_out(s, j, q).start()

    def forward_pieces(s):
        for q in range(4):
            for j in (2, 1, 3):
                ysend[s, j, q] = partial_of(s, (y + j) % 4, q).astype(BF16)
                y_out(s, j, q).start()
            own[q] = partial_of(s, y, q)

    def middle(s):
        for kd in range(2):
            own[2 * zh + kd] = own[2 * zh + kd] - traw[kd, s].astype(F32).T
        for q in range(4):
            total = own[q]
            for j in (1, 3, 2):
                y_out(s, j, q).wait_recv()
                total = total + yrecv[s, j, q].astype(F32)
            ysum[q] = total
            zsend[s, q] = total.astype(BF16)
            z_out(s, q).start()
        for q in range(4):
            z_out(s, q).wait_recv()
            resid[s, y, q] = (ysum[q] + zrecv[s, q].astype(F32)).astype(BF16)
            for j in (2, 1, 3):
                g_out(s, j, q).start()

    def backward_own(s):
        r = jnp.concatenate([resid[s, y, q] for q in range(4)], axis=1)
        for kd in range(2):
            grad[:, kd * BLOCK : (kd + 1) * BLOCK] = dot_nn(r, xg[s, y, kd])

    def backward(s):
        for h in range(2):
            for j in (1, 3, 2):
                b = (y + 4 - j) % 4
                for q in (2 * h, 2 * h + 1):
                    g_from(s, j, q).wait_recv()
                r = jnp.concatenate([resid[s, b, 2 * h], resid[s, b, 2 * h + 1]], axis=1)
                for kd in range(2):
                    grad[:, kd * BLOCK : (kd + 1) * BLOCK] += dot_nn(r, xg[s, b, kd, halves[h], :])

    pieces = [(h, c) for c in range(4) for h in range(2)]

    def columns(h, c):
        return slice(h * BLOCK + c * PART, h * BLOCK + (c + 1) * PART)

    def update(s, then):
        power = PRIOR + s + 1
        for h, c in pieces:
            for cut in range(2):
                part = (slice(cut * 64, cut * 64 + 64), columns(h, c))
                gradient = grad[part] * (1.0 / TOKENS)
                first = beta_first * mt[part] + (1.0 - beta_first) * gradient
                second = beta_second * vt[part] + (1.0 - beta_second) * gradient * gradient
                corrected = (
                    first
                    / (1.0 - beta_first**power)
                    / (jnp.sqrt(second / (1.0 - beta_second**power)) + epsilon_value)
                )
                old = wt[part]
                new = old - inner_rate * (corrected + decay_rate * old)
                mt[part] = first
                vt[part] = second
                wt[part] = new
                if s + 1 < STEPS:
                    wb[part] = new.astype(BF16)
            then(h, c)

    def x_arrived(s, d):
        for h in range(2):
            x_sib(s, d, h, incoming=True).wait_recv()

    fast = g < 3
    total_steps = float(3 * STEPS + SLOW_STEPS)
    weight = jnp.where(fast, float(STEPS), float(SLOW_STEPS)) / total_steps

    def adder(h):
        return at(1 + h, y, zh)

    def slow_out(h):
        return remote(slow.at[h], slow_in, os_.at[h], or_, adder(h))

    way_in = jnp.where(g == 0, 0, 1)

    def early_out(h):
        return remote(early.at[h], early_in.at[way_in], es.at[h], er.at[way_in], adder(h))

    def early_from(i):
        return remote(early.at[0], early_in.at[i], es.at[0], er.at[i], adder(0))

    half = jnp.where(g == 2, 1, 0)
    adds = jnp.logical_or(g == 1, g == 2)

    def early_sum_out(j):
        return remote(early_sum.at[half], early_sum.at[half], as_.at[j], ar.at[half], gdev(j))

    def early_sum_from(h):
        return remote(early_sum.at[h], early_sum.at[h], as_.at[1], ar.at[h], gdev(1))

    def late_out(h, c):
        return remote(late.at[h, c], late_in.at[way_in, c], ls.at[h, c], lr.at[way_in, c], adder(h))

    def late_from(i, c):
        return remote(late.at[0, c], late_in.at[i, c], ls.at[0, c], lr.at[i, c], adder(0))

    def late_sum_out(j, c):
        return remote(late_sum.at[half, c], late_sum.at[half, c], fs.at[j, c], fr.at[half, c], gdev(j))

    def late_sum_from(h, c):
        return remote(late_sum.at[h, c], late_sum.at[h, c], fs.at[1, c], fr.at[h, c], gdev(1))

    def moved(h, c):
        return weight * (ot[:, columns(h, c)] - wt[:, columns(h, c)])

    def nothing(h, c):
        return None

    def to_slow(h, c):
        slow[h, c] = moved(h, c)

    def to_early(h, c):
        early[h, c] = moved(h, c).astype(BF16)
        if c == 3:

            @pl.when(g != 1 + h)
            def _():
                early_out(h).start()

    def to_late(h, c):
        late[h, c] = (moved(h, c) - early[h, c].astype(F32)).astype(BF16)

        @pl.when(g != 1 + h)
        def _():
            late_out(h, c).start()

    locals_[1].wait()
    x_arrived(0, 0)
    forward_block(0, x)
    x_middle(0)
    x_arrived(0, 3)
    forward_block(0, xl)
    x_arrived(0, 1)
    forward_block(0, xr_)
    x_end(0)

    @pl.when(fast)
    def _():
        x_begin(1)

    locals_[6].wait()
    t_swap(1 - k).wait_recv()
    x_arrived(0, 2)
    forward_block(0, xo)
    middle(0)

    @pl.when(fast)
    def _():
        x_middle(1)

    backward_own(0)
    backward(0)
    update(0, nothing)

    locals_[2].wait()
    locals_[3].wait()

    @pl.when(jnp.logical_not(fast))
    def _():
        for h, c in pieces:
            to_slow(h, c)
        for h in range(2):
            slow_out(h).start()

    @pl.when(fast)
    def _():
        for s in range(1, STEPS):
            x_end(s)
            if s + 1 < STEPS:
                x_begin(s + 1)
            for d in (0, 3, 1, 2):
                x_arrived(s, d)
            forward_pieces(s)
            middle(s)
            if s + 1 < STEPS:
                x_middle(s + 1)
            backward_own(s)
            if s + 1 == STEPS:

                @pl.when(adds)
                def _():
                    for i in range(2):
                        early_from(i).wait_recv()
                    slow_out(0).wait_recv()
                    for c in range(4):
                        total = early[half, c].astype(F32) + slow_in[c]
                        for i in range(2):
                            total = total + early_in[i, c].astype(F32)
                        rounded = total.astype(BF16)
                        early_sum[half, c] = rounded
                        left_over[c] = total - rounded.astype(F32)
                    for j in (2, 1, 3):
                        early_sum_out(j).start()

            backward(s)
            update(s, (nothing, to_early, to_late)[s])

    @pl.when(adds)
    def _():
        for c in range(4):
            total = late[half, c].astype(F32) + left_over[c]
            for i in range(2):
                late_from(i, c).wait_recv()
                total = total + late_in[i, c].astype(F32)
            late_sum[half, c] = total.astype(BF16)
            for j in (2, 1, 3):
                late_sum_out(j, c).start()

    for h in range(2):

        @pl.when(g != 1 + h)
        def _():
            early_sum_from(h).wait_recv()

    def away(c):
        return remote(stage.at[1 - k, c], back.at[c], bs.at[c], br.at[c], sib)

    for c in range(4):
        for h in range(2):

            @pl.when(g != 1 + h)
            def _():
                late_sum_from(h, c).wait_recv()

            stage[h, c] = (early_sum[h, c].astype(F32) + late_sum[h, c].astype(F32)).T
        away(c).start()
    for c in range(4):
        away(c).wait_recv()
        here = slice(c * PART, (c + 1) * PART)

        @pl.when(role == 0)
        def _():
            o_ref[here, :PART] = stage[k, c]
            o_ref[here, PART:] = back[c]

        @pl.when(role == 1)
        def _():
            o_ref[here, :PART] = back[c]
            o_ref[here, PART:] = stage[k, c]

    for c in range(4):
        away(c).wait_send()
    for i in range(3):
        swap_in(i).wait_send()
    t_swap(k).wait_send()

    @pl.when(adds)
    def _():
        for j in (1, 2, 3):
            early_sum_out(j).wait_send()
            for c in range(4):
                late_sum_out(j, c).wait_send()

    def sent(s):
        for way in range(2):
            for h in range(2):
                x_own(s, h, way).wait_send()
            x_fwd(s, way).wait_send()
        for d in range(4):
            for h in range(2):
                x_sib(s, d, h).wait_send()
        for q in range(4):
            for j in (1, 2, 3):
                y_out(s, j, q).wait_send()
                g_out(s, j, q).wait_send()
            z_out(s, q).wait_send()

    sent(0)

    @pl.when(jnp.logical_not(fast))
    def _():
        for h in range(2):
            slow_out(h).wait_send()

    @pl.when(fast)
    def _():
        for s in range(1, STEPS):
            sent(s)
        for h in range(2):

            @pl.when(g != 1 + h)
            def _():
                early_out(h).wait_send()
                for c in range(4):
                    late_out(h, c).wait_send()


def pseudo_of(outer_params, first_moment, second_moment, activations, targets):
    dma = pltpu.SemaphoreType.DMA
    vm = pltpu.VMEM
    hbm = pl.BlockSpec(memory_space=pltpu.HBM)
    n = STEPS
    tile = (PART, PART)
    return pl.pallas_call(
        kernel,
        out_shape=jax.ShapeDtypeStruct((512, 256), F32),
        in_specs=[hbm] * 5,
        out_specs=pl.BlockSpec(memory_space=pltpu.VMEM),
        scratch_shapes=[
            vm((n, 4, 2, 512, 512), BF16),
            vm((3, 2, 512, PART), F32),
            vm((PART, 1024), F32), vm((PART, 1024), F32), vm((PART, 1024), F32), vm((PART, 1024), F32),
            vm((PART, 1024), BF16),
            vm((2, n, *tile), BF16),
            vm((4, *tile), F32),
            vm((n, 4, 4, *tile), BF16), vm((n, 4, 4, *tile), BF16),
            vm((4, *tile), F32),
            vm((n, 4, *tile), BF16), vm((n, 4, *tile), BF16),
            vm((n, 4, 4, *tile), BF16),
            vm((PART, 1024), F32),
            vm((2, 4, *tile), F32), vm((4, *tile), F32),
            vm((2, 4, *tile), BF16), vm((2, 4, *tile), BF16), vm((2, 4, *tile), BF16),
            vm((4, *tile), F32),
            vm((2, 4, *tile), BF16), vm((2, 4, *tile), BF16), vm((2, 4, *tile), BF16),
            vm((2, 4, *tile), F32), vm((4, *tile), F32),
            dma((7,)),
            dma((n, 6)), dma((n, 6)), dma((n, 8)), dma((n, 8)),
            dma((3,)), dma((3,)), dma, dma,
            dma((n, 4, 4)), dma((n, 4, 4)), dma((n, 4)), dma((n, 4)),
            dma((n, 4, 4)), dma((n, 4, 4)),
            dma((2,)), dma, dma((2,)), dma((2,)), dma((4,)), dma((2,)),
            dma((2, 4)), dma((2, 4)), dma((4, 4)), dma((2, 4)),
            dma((4,)), dma((4,)),
        ],
        compiler_params=pltpu.CompilerParams(
            collective_id=0, has_side_effects=True, vmem_limit_bytes=63 << 20
        ),
    )(outer_params, first_moment, second_moment, activations, targets)


def local(outer_params, first_moment, second_moment, outer_moment, activations, targets):
    pseudo = pseudo_of(outer_params, first_moment, second_moment, activations, targets)
    new_moment = momentum_coef * outer_moment + pseudo
    new_params = outer_params - outer_rate * (pseudo + momentum_coef * new_moment)
    return (new_params, new_moment)


def solution(mesh):
    placed = (
        P("col", "row"),
        P("grp", "col", "row"),
        P("grp", "col", "row"),
        P("col", "row"),
        P("grp", None, "row", "col"),
        P("grp", None, "col", "row"),
    )
    return jax.shard_map(
        local,
        mesh=mesh,
        in_specs=placed,
        out_specs=(P("col", "row"), P("col", "row")),
        check_vma=False,
    )
```

```python
import functools

import jax
import jax.numpy as jnp
from jax import lax
from jax.experimental import pallas as pl
from jax.experimental.pallas import tpu as pltpu
from jax.sharding import PartitionSpec as P

TOKENS = 2048
STEPS = 3
SLOW_STEPS = 1
PRIOR = 100
BLOCK = 512
PART = 128
CUTS = (1, 1, 1, 1)

beta_first = 0.9
beta_second = 0.95
inner_rate = 0.01
decay_rate = 0.1
epsilon_value = 1e-08
outer_rate = 0.7
momentum_coef = 0.9

F32 = jnp.float32
BF16 = jnp.bfloat16


def dot_nt(a, b):
    return lax.dot_general(a, b, (((1,), (1,)), ((), ())), preferred_element_type=F32)


def dot_nn(a, b):
    return lax.dot_general(a, b, (((1,), (0,)), ((), ())), preferred_element_type=F32)


def kernel(
    w_in, m_in, v_in, x_in, t_in, o_ref,
    xg, raw, wt, mt, vt, ot, wb, traw, own, ysend, yrecv, ysum, zsend, zrecv, resid, grad,
    slow, slow_in, early, early_in, early_sum, left_over, late, late_in, late_sum, stage, back,
    lsem, xs, xr, ss, sr, ws, wr, ts, tr, ys, yr, zs, zr, gs, gr,
    os_, or_, es, er, as_, ar, ls, lr, fs, fr, bs, br,
):
    g = lax.axis_index("grp")
    x = lax.axis_index("row")
    col = lax.axis_index("col")
    y = col // 4
    zh = (col // 2) % 2
    k = col % 2

    def flip(g_, y_, zh_):
        return (y_ // 2 + zh_ + g_) % 2

    role = (k + flip(g, y, zh)) % 2

    def at(g_, y_, zh_):
        return {"grp": g_, "col": y_ * 4 + zh_ * 2 + (role + flip(g_, y_, zh_)) % 2}

    sib = {"col": y * 4 + zh * 2 + (1 - k)}
    zdev = at(g, y, 1 - zh)
    across = y * 4 + zh * 2 + (1 - k)
    right = {"row": (x + 1) % 4, "col": across}
    left = {"row": (x + 3) % 4, "col": across}
    xl, xr_, xo = (x + 3) % 4, (x + 1) % 4, (x + 2) % 4

    def ydev(j):
        return at(g, (y + j) % 4, zh)

    def gdev(j):
        return at((g + j) % 4, y, zh)

    def remote(src, dst, s_sem, r_sem, dev):
        return pltpu.make_async_remote_copy(
            src_ref=src, dst_ref=dst, send_sem=s_sem, recv_sem=r_sem,
            device_id=dev, device_id_type=pl.DeviceIdType.MESH,
        )

    barrier = pltpu.get_barrier_semaphore()
    peers = [sib, right, left, zdev] + [ydev(j) for j in (1, 2, 3)] + [gdev(j) for j in (1, 2, 3)]
    for dev in peers:
        pl.semaphore_signal(barrier, inc=1, device_id=dev, device_id_type=pl.DeviceIdType.MESH)

    mine = pl.ds(pl.multiple_of(role * PART, PART), PART)
    other = pl.ds(pl.multiple_of((1 - role) * PART, PART), PART)
    locals_ = [pltpu.make_async_copy(w_in.at[:, mine], raw.at[0, k], lsem.at[0])]
    locals_ += [pltpu.make_async_copy(x_in.at[0, s], xg.at[s, x, k], lsem.at[1 + s]) for s in range(STEPS)]
    locals_ += [pltpu.make_async_copy(m_in.at[0, :, mine], raw.at[1, k], lsem.at[4])]
    locals_ += [pltpu.make_async_copy(v_in.at[0, :, mine], raw.at[2, k], lsem.at[5])]
    locals_ += [pltpu.make_async_copy(t_in.at[0, :, :, mine], traw.at[k], lsem.at[6])]
    for c in locals_:
        c.start()

    pl.semaphore_wait(barrier, len(peers))

    halves = (pl.ds(0, 256), pl.ds(256, 256))

    def x_copy(s, slot, src, dst, way):
        return remote(src, dst, xs.at[s, slot], xr.at[s, slot], (right, left)[way])

    def x_own(s, h, way):
        return x_copy(s, 2 * way + h, x_in.at[0, s, halves[h]], xg.at[s, x, k, halves[h]], way)

    def x_from(s, h, way):
        here = xg.at[s, (xl, xr_)[way], 1 - k, halves[h]]
        return x_copy(s, 2 * way + h, here, here, way)

    def x_fwd(s, way):
        here = xg.at[s, (xl, xr_)[way], 1 - k, halves[way]]
        return x_copy(s, 4 + way, here, here, way)

    def x_opp(s, way):
        here = xg.at[s, xo, k, halves[way]]
        return x_copy(s, 4 + way, here, here, way)

    def x_sib(s, d, h, src=None, incoming=False):
        kd = (k + d + incoming) % 2
        here = xg.at[s, (x + d) % 4, kd, halves[h]]
        return remote(here if src is None else src, here, ss.at[s, 2 * d + h], sr.at[s, 2 * d + h], sib)

    def x_begin(s):
        x_own(s, 0, 0).start()
        x_own(s, 1, 1).start()
        x_own(s, 1, 0).start()
        x_own(s, 0, 1).start()
        for h in range(2):
            x_sib(s, 0, h, x_in.at[0, s, halves[h]]).start()

    def x_middle(s):
        x_from(s, 0, 0).wait_recv()
        x_fwd(s, 0).start()
        x_sib(s, 3, 0).start()
        x_from(s, 1, 1).wait_recv()
        x_fwd(s, 1).start()
        x_sib(s, 1, 1).start()

    def x_rest(s):
        x_from(s, 1, 0).wait_recv()
        x_sib(s, 3, 1).start()
        x_from(s, 0, 1).wait_recv()
        x_sib(s, 1, 0).start()

    def x_end(s):
        for way in range(2):
            x_opp(s, way).wait_recv()
            x_sib(s, 2, way).start()

    def swap(i, ref):
        return remote(ref, raw.at[i, k], ws.at[i], wr.at[i], sib)

    def swap_in(i):
        return remote(raw.at[i, 1 - k], raw.at[i, 1 - k], ws.at[i], wr.at[i], sib)

    def t_swap(kd):
        return remote(t_in.at[0, :, :, other], traw.at[kd], ts, tr, sib)

    swap(0, w_in.at[:, other]).start()
    x_begin(0)
    swap(1, m_in.at[0, :, other]).start()
    swap(2, v_in.at[0, :, other]).start()
    t_swap(k).start()

    def turned(i, dst):
        for kd in range(2):
            for r in range(4):
                dst[:, kd * BLOCK + r * PART : kd * BLOCK + (r + 1) * PART] = raw[
                    i, kd, r * PART : (r + 1) * PART, :
                ].T

    locals_[0].wait()
    swap_in(0).wait_recv()
    turned(0, wt)
    ot[...] = wt[...]
    wb[...] = wt[...].astype(BF16)
    locals_[4].wait()
    locals_[5].wait()
    swap_in(1).wait_recv()
    turned(1, mt)
    swap_in(2).wait_recv()
    turned(2, vt)

    def partial_of(s, b, q):
        rows = pl.ds(q * PART, PART)
        return dot_nt(wb[:, :BLOCK], xg[s, b, 0, rows, :]) + dot_nt(wb[:, BLOCK:], xg[s, b, 1, rows, :])

    def cuts(q):
        height = PART // CUTS[q]
        return [(i, slice(i * height, (i + 1) * height)) for i in range(CUTS[q])]

    def y_out(s, j, q, i, rows):
        here, there = ysend.at[s, j, q, rows], yrecv.at[s, j, q, rows]
        return remote(here, there, ys.at[s, j, q, i], yr.at[s, j, q, i], ydev(j))

    def z_out(s, q, i, rows):
        return remote(zsend.at[s, q, rows], zrecv.at[s, q, rows], zs.at[s, q, i], zr.at[s, q, i], zdev)

    def g_copy(s, b, j, q, i, rows):
        here = resid.at[s, b, q, rows]
        return remote(here, here, gs.at[s, j, q, i], gr.at[s, j, q, i], ydev(j))

    def g_out(s, j, q, i, rows):
        return g_copy(s, y, j, q, i, rows)

    def g_from(s, j, q, i, rows):
        return g_copy(s, (y + 4 - j) % 4, j, q, i, rows)

    def forward_block(s, b):
        j = (b + 4 - y) % 4
        for q in range(4):
            value = partial_of(s, b, q)

            @pl.when(j == 0)
            def _():
                own[q] = value

            @pl.when(j != 0)
            def _():
                ysend[s, j, q] = value.astype(BF16)
                for cut in cuts(q):
                    y_out(s, j, q, *cut).start()

    def forward_pieces(s):
        for q in range(4):
            for j in (2, 1, 3):
                ysend[s, j, q] = partial_of(s, (y + j) % 4, q).astype(BF16)
                y_out(s, j, q, *cuts(q)[0]).start()
            for cut in cuts(q)[1:]:
                for j in (2, 1, 3):
                    y_out(s, j, q, *cut).start()
            own[q] = partial_of(s, y, q)

    def gather_y(s):
        for kd in range(2):
            own[2 * zh + kd] = own[2 * zh + kd] - traw[kd, s].astype(F32).T
        for q in range(4):
            for i, rows in cuts(q):
                total = own[q, rows]
                for j in (1, 3, 2):
                    y_out(s, j, q, i, rows).wait_recv()
                    total = total + yrecv[s, j, q, rows].astype(F32)
                ysum[q, rows] = total
                zsend[s, q, rows] = total.astype(BF16)
                z_out(s, q, i, rows).start()

    def gather_z(s):
        for q in range(4):
            for i, rows in cuts(q):
                z_out(s, q, i, rows).wait_recv()
                resid[s, y, q, rows] = (ysum[q, rows] + zrecv[s, q, rows].astype(F32)).astype(BF16)
                for j in (2, 1, 3):
                    g_out(s, j, q, i, rows).start()

    def backward_own(s):
        r = jnp.concatenate([resid[s, y, q] for q in range(4)], axis=1)
        for kd in range(2):
            grad[:, kd * BLOCK : (kd + 1) * BLOCK] = dot_nn(r, xg[s, y, kd])

    def backward(s):
        for h in range(2):
            for j in (1, 3, 2):
                b = (y + 4 - j) % 4
                for q in (2 * h, 2 * h + 1):
                    for cut in cuts(q):
                        g_from(s, j, q, *cut).wait_recv()
                r = jnp.concatenate([resid[s, b, 2 * h], resid[s, b, 2 * h + 1]], axis=1)
                for kd in range(2):
                    grad[:, kd * BLOCK : (kd + 1) * BLOCK] += dot_nn(r, xg[s, b, kd, halves[h], :])

    pieces = [(h, c) for c in range(4) for h in range(2)]

    def columns(h, c):
        return slice(h * BLOCK + c * PART, h * BLOCK + (c + 1) * PART)

    def update(s, then):
        power = PRIOR + s + 1
        for h, c in pieces:
            for cut in range(2):
                part = (slice(cut * 64, cut * 64 + 64), columns(h, c))
                gradient = grad[part] * (1.0 / TOKENS)
                first = beta_first * mt[part] + (1.0 - beta_first) * gradient
                second = beta_second * vt[part] + (1.0 - beta_second) * gradient * gradient
                corrected = (
                    first
                    / (1.0 - beta_first**power)
                    / (jnp.sqrt(second / (1.0 - beta_second**power)) + epsilon_value)
                )
                old = wt[part]
                new = old - inner_rate * (corrected + decay_rate * old)
                mt[part] = first
                vt[part] = second
                wt[part] = new
                if s + 1 < STEPS:
                    wb[part] = new.astype(BF16)
            then(h, c)

    def x_arrived(s, d):
        for h in range(2):
            x_sib(s, d, h, incoming=True).wait_recv()

    def sent(s):
        for way in range(2):
            for h in range(2):
                x_own(s, h, way).wait_send()
            x_fwd(s, way).wait_send()
        for d in range(4):
            for h in range(2):
                x_sib(s, d, h).wait_send()
        for q in range(4):
            for cut in cuts(q):
                for j in (1, 2, 3):
                    y_out(s, j, q, *cut).wait_send()
                    g_out(s, j, q, *cut).wait_send()
                z_out(s, q, *cut).wait_send()

    fast = g < 3
    total_steps = float(3 * STEPS + SLOW_STEPS)
    weight = jnp.where(fast, float(STEPS), float(SLOW_STEPS)) / total_steps

    def adder(h):
        return at(1 + h, y, zh)

    def slow_out(h):
        return remote(slow.at[h], slow_in, os_.at[h], or_, adder(h))

    way_in = jnp.where(g == 0, 0, 1)

    def early_out(h):
        return remote(early.at[h], early_in.at[way_in], es.at[h], er.at[way_in], adder(h))

    def early_from(i):
        return remote(early.at[0], early_in.at[i], es.at[0], er.at[i], adder(0))

    half = jnp.where(g == 2, 1, 0)
    adds = jnp.logical_or(g == 1, g == 2)

    def early_sum_out(j):
        return remote(early_sum.at[half], early_sum.at[half], as_.at[j], ar.at[half], gdev(j))

    def early_sum_from(h):
        return remote(early_sum.at[h], early_sum.at[h], as_.at[1], ar.at[h], gdev(1))

    def late_out(h, c):
        return remote(late.at[h, c], late_in.at[way_in, c], ls.at[h, c], lr.at[way_in, c], adder(h))

    def late_from(i, c):
        return remote(late.at[0, c], late_in.at[i, c], ls.at[0, c], lr.at[i, c], adder(0))

    def late_sum_out(j, c):
        return remote(late_sum.at[half, c], late_sum.at[half, c], fs.at[j, c], fr.at[half, c], gdev(j))

    def late_sum_from(h, c):
        return remote(late_sum.at[h, c], late_sum.at[h, c], fs.at[1, c], fr.at[h, c], gdev(1))

    def moved(h, c):
        return weight * (ot[:, columns(h, c)] - wt[:, columns(h, c)])

    def nothing(h, c):
        return None

    def to_slow(h, c):
        slow[h, c] = moved(h, c)

    def to_early(h, c):
        early[h, c] = moved(h, c).astype(BF16)
        if c == 3:

            @pl.when(g != 1 + h)
            def _():
                early_out(h).start()

    def to_late(h, c):
        late[h, c] = (moved(h, c) - early[h, c].astype(F32)).astype(BF16)

        @pl.when(g != 1 + h)
        def _():
            late_out(h, c).start()

    locals_[1].wait()
    x_arrived(0, 0)
    forward_block(0, x)
    x_middle(0)
    x_rest(0)
    x_arrived(0, 3)
    forward_block(0, xl)
    x_arrived(0, 1)
    forward_block(0, xr_)

    @pl.when(fast)
    def _():
        x_begin(1)

    x_end(0)
    locals_[6].wait()
    t_swap(1 - k).wait_recv()
    x_arrived(0, 2)
    forward_block(0, xo)
    gather_y(0)

    @pl.when(fast)
    def _():
        x_middle(1)

    gather_z(0)
    backward_own(0)

    @pl.when(fast)
    def _():
        x_rest(1)

    backward(0)
    update(0, nothing)

    locals_[2].wait()
    locals_[3].wait()

    @pl.when(jnp.logical_not(fast))
    def _():
        for h, c in pieces:
            to_slow(h, c)
        for h in range(2):
            slow_out(h).start()
        sent(0)
        for i in range(3):
            swap_in(i).wait_send()
        t_swap(k).wait_send()
        for h in range(2):
            slow_out(h).wait_send()

    @pl.when(fast)
    def _():
        for s in range(1, STEPS):
            x_end(s)
            if s + 1 < STEPS:
                x_begin(s + 1)
            for d in (0, 3, 1, 2):
                x_arrived(s, d)
            forward_pieces(s)
            sent(s - 1)
            if s == 1:
                for i in range(3):
                    swap_in(i).wait_send()
                t_swap(k).wait_send()
            gather_y(s)
            if s + 1 < STEPS:
                x_middle(s + 1)
            gather_z(s)
            backward_own(s)
            if s + 1 < STEPS:
                x_rest(s + 1)
            if s + 1 == STEPS:

                @pl.when(adds)
                def _():
                    for i in range(2):
                        early_from(i).wait_recv()
                    slow_out(0).wait_recv()
                    for c in range(4):
                        total = early[half, c].astype(F32) + slow_in[c]
                        for i in range(2):
                            total = total + early_in[i, c].astype(F32)
                        rounded = total.astype(BF16)
                        early_sum[half, c] = rounded
                        left_over[c] = total - rounded.astype(F32)
                    for j in (2, 1, 3):
                        early_sum_out(j).start()

            backward(s)
            update(s, (nothing, to_early, to_late)[s])

    @pl.when(adds)
    def _():
        for c in range(4):
            total = late[half, c].astype(F32) + left_over[c]
            for i in range(2):
                late_from(i, c).wait_recv()
                total = total + late_in[i, c].astype(F32)
            late_sum[half, c] = total.astype(BF16)
            for j in (2, 1, 3):
                late_sum_out(j, c).start()

    @pl.when(fast)
    def _():
        sent(STEPS - 1)
        for h in range(2):

            @pl.when(g != 1 + h)
            def _():
                early_out(h).wait_send()
                for c in range(4):
                    late_out(h, c).wait_send()

    @pl.when(adds)
    def _():
        for j in (1, 2, 3):
            early_sum_out(j).wait_send()

    for h in range(2):

        @pl.when(g != 1 + h)
        def _():
            early_sum_from(h).wait_recv()

    def away(c):
        return remote(stage.at[1 - k, c], back.at[c], bs.at[c], br.at[c], sib)

    for c in range(4):
        for h in range(2):

            @pl.when(g != 1 + h)
            def _():
                late_sum_from(h, c).wait_recv()

            stage[h, c] = (early_sum[h, c].astype(F32) + late_sum[h, c].astype(F32)).T
        away(c).start()
    for c in range(4):
        away(c).wait_recv()
        here = slice(c * PART, (c + 1) * PART)

        @pl.when(role == 0)
        def _():
            o_ref[here, :PART] = stage[k, c]
            o_ref[here, PART:] = back[c]

        @pl.when(role == 1)
        def _():
            o_ref[here, :PART] = back[c]
            o_ref[here, PART:] = stage[k, c]

    for c in range(4):
        away(c).wait_send()

    @pl.when(adds)
    def _():
        for j in (1, 2, 3):
            for c in range(4):
                late_sum_out(j, c).wait_send()


def pseudo_of(outer_params, first_moment, second_moment, activations, targets):
    dma = pltpu.SemaphoreType.DMA
    vm = pltpu.VMEM
    hbm = pl.BlockSpec(memory_space=pltpu.HBM)
    n = STEPS
    tile = (PART, PART)
    return pl.pallas_call(
        kernel,
        out_shape=jax.ShapeDtypeStruct((512, 256), F32),
        in_specs=[hbm] * 5,
        out_specs=pl.BlockSpec(memory_space=pltpu.VMEM),
        scratch_shapes=[
            vm((n, 4, 2, 512, 512), BF16),
            vm((3, 2, 512, PART), F32),
            vm((PART, 1024), F32), vm((PART, 1024), F32), vm((PART, 1024), F32), vm((PART, 1024), F32),
            vm((PART, 1024), BF16),
            vm((2, n, *tile), BF16),
            vm((4, *tile), F32),
            vm((n, 4, 4, *tile), BF16), vm((n, 4, 4, *tile), BF16),
            vm((4, *tile), F32),
            vm((n, 4, *tile), BF16), vm((n, 4, *tile), BF16),
            vm((n, 4, 4, *tile), BF16),
            vm((PART, 1024), F32),
            vm((2, 4, *tile), F32), vm((4, *tile), F32),
            vm((2, 4, *tile), BF16), vm((2, 4, *tile), BF16), vm((2, 4, *tile), BF16),
            vm((4, *tile), F32),
            vm((2, 4, *tile), BF16), vm((2, 4, *tile), BF16), vm((2, 4, *tile), BF16),
            vm((2, 4, *tile), F32), vm((4, *tile), F32),
            dma((7,)),
            dma((n, 6)), dma((n, 6)), dma((n, 8)), dma((n, 8)),
            dma((3,)), dma((3,)), dma, dma,
            dma((n, 4, 4, max(CUTS))), dma((n, 4, 4, max(CUTS))), dma((n, 4, max(CUTS))), dma((n, 4, max(CUTS))),
            dma((n, 4, 4, max(CUTS))), dma((n, 4, 4, max(CUTS))),
            dma((2,)), dma, dma((2,)), dma((2,)), dma((4,)), dma((2,)),
            dma((2, 4)), dma((2, 4)), dma((4, 4)), dma((2, 4)),
            dma((4,)), dma((4,)),
        ],
        compiler_params=pltpu.CompilerParams(
            collective_id=0, has_side_effects=True, vmem_limit_bytes=63 << 20
        ),
    )(outer_params, first_moment, second_moment, activations, targets)


def local(outer_params, first_moment, second_moment, outer_moment, activations, targets):
    pseudo = pseudo_of(outer_params, first_moment, second_moment, activations, targets)
    new_moment = momentum_coef * outer_moment + pseudo
    new_params = outer_params - outer_rate * (pseudo + momentum_coef * new_moment)
    return (new_params, new_moment)


def solution(mesh):
    placed = (
        P("col", "row"),
        P("grp", "col", "row"),
        P("grp", "col", "row"),
        P("col", "row"),
        P("grp", None, "row", "col"),
        P("grp", None, "col", "row"),
    )
    return jax.shard_map(
        local,
        mesh=mesh,
        in_specs=placed,
        out_specs=(P("col", "row"), P("col", "row")),
        check_vma=False,
    )
```

```python
import functools

import jax
import jax.numpy as jnp
from jax import lax
from jax.experimental import pallas as pl
from jax.experimental.pallas import tpu as pltpu
from jax.sharding import PartitionSpec as P

TOKENS = 2048
STEPS = 3
SLOW_STEPS = 1
PRIOR = 100
BLOCK = 512
PART = 128

beta_first = 0.9
beta_second = 0.95
inner_rate = 0.01
decay_rate = 0.1
epsilon_value = 1e-08
outer_rate = 0.7
momentum_coef = 0.9

F32 = jnp.float32
BF16 = jnp.bfloat16


def dot_nt(a, b):
    return lax.dot_general(a, b, (((1,), (1,)), ((), ())), preferred_element_type=F32)


def dot_nn(a, b):
    return lax.dot_general(a, b, (((1,), (0,)), ((), ())), preferred_element_type=F32)


def kernel(
    w_in, m_in, v_in, x_in, t_in, o_ref,
    xg, raw, wt, mt, vt, ot, wb, traw, own, ysend, yrecv, ysum, zsend, zrecv, resid, grad,
    slow, slow_in, early, early_in, early_sum, left_over, late, late_in, late_sum, stage, back,
    lsem, xs, xr, ss, sr, ws, wr, ts, tr, ys, yr, zs, zr, gs, gr,
    os_, or_, es, er, as_, ar, ls, lr, fs, fr, bs, br,
):
    g = lax.axis_index("grp")
    x = lax.axis_index("row")
    col = lax.axis_index("col")
    y = col // 4
    zh = (col // 2) % 2
    k = col % 2

    def flip(g_, y_, zh_):
        return (y_ // 2 + zh_ + g_) % 2

    role = (k + flip(g, y, zh)) % 2

    def at(g_, y_, zh_):
        return {"grp": g_, "col": y_ * 4 + zh_ * 2 + (role + flip(g_, y_, zh_)) % 2}

    sib = {"col": y * 4 + zh * 2 + (1 - k)}
    zdev = at(g, y, 1 - zh)
    across = y * 4 + zh * 2 + (1 - k)
    right = {"row": (x + 1) % 4, "col": across}
    left = {"row": (x + 3) % 4, "col": across}
    xl, xr_, xo = (x + 3) % 4, (x + 1) % 4, (x + 2) % 4

    def ydev(j):
        return at(g, (y + j) % 4, zh)

    def core_of(role_, y_):
        return {"col": y_ * 4 + zh * 2 + (role_ + flip(g, y_, zh)) % 2}

    def gdev(j):
        return at((g + j) % 4, y, zh)

    def remote(src, dst, s_sem, r_sem, dev):
        return pltpu.make_async_remote_copy(
            src_ref=src, dst_ref=dst, send_sem=s_sem, recv_sem=r_sem,
            device_id=dev, device_id_type=pl.DeviceIdType.MESH,
        )

    barrier = pltpu.get_barrier_semaphore()
    peers = [sib, right, left, zdev] + [ydev(j) for j in (1, 2, 3)] + [gdev(j) for j in (1, 2, 3)]
    peers += [core_of(1 - role, (y + j) % 4) for j in (1, 2, 3)]
    for dev in peers:
        pl.semaphore_signal(barrier, inc=1, device_id=dev, device_id_type=pl.DeviceIdType.MESH)

    mine = pl.ds(pl.multiple_of(role * PART, PART), PART)
    other = pl.ds(pl.multiple_of((1 - role) * PART, PART), PART)
    locals_ = [pltpu.make_async_copy(w_in.at[:, mine], raw.at[0, k], lsem.at[0])]
    locals_ += [pltpu.make_async_copy(x_in.at[0, s], xg.at[s, x, k], lsem.at[1 + s]) for s in range(STEPS)]
    locals_ += [pltpu.make_async_copy(m_in.at[0, :, mine], raw.at[1, k], lsem.at[4])]
    locals_ += [pltpu.make_async_copy(v_in.at[0, :, mine], raw.at[2, k], lsem.at[5])]
    for c in locals_:
        c.start()

    pl.semaphore_wait(barrier, len(peers))

    halves = (pl.ds(0, 256), pl.ds(256, 256))

    def x_copy(s, slot, src, dst, way):
        return remote(src, dst, xs.at[s, slot], xr.at[s, slot], (right, left)[way])

    def x_own(s, h, way):
        return x_copy(s, 2 * way + h, x_in.at[0, s, halves[h]], xg.at[s, x, k, halves[h]], way)

    def x_from(s, h, way):
        here = xg.at[s, (xl, xr_)[way], 1 - k, halves[h]]
        return x_copy(s, 2 * way + h, here, here, way)

    def x_fwd(s, way):
        here = xg.at[s, (xl, xr_)[way], 1 - k, halves[way]]
        return x_copy(s, 4 + way, here, here, way)

    def x_opp(s, way):
        here = xg.at[s, xo, k, halves[way]]
        return x_copy(s, 4 + way, here, here, way)

    def x_sib(s, d, h, src=None, incoming=False):
        kd = (k + d + incoming) % 2
        here = xg.at[s, (x + d) % 4, kd, halves[h]]
        return remote(here if src is None else src, here, ss.at[s, 2 * d + h], sr.at[s, 2 * d + h], sib)

    def x_begin(s):
        x_own(s, 0, 0).start()
        x_own(s, 1, 1).start()
        x_own(s, 1, 0).start()
        x_own(s, 0, 1).start()
        for h in range(2):
            x_sib(s, 0, h, x_in.at[0, s, halves[h]]).start()

    def x_middle(s):
        x_from(s, 0, 0).wait_recv()
        x_fwd(s, 0).start()
        x_sib(s, 3, 0).start()
        x_from(s, 1, 1).wait_recv()
        x_fwd(s, 1).start()
        x_sib(s, 1, 1).start()

    def x_rest(s):
        x_from(s, 1, 0).wait_recv()
        x_sib(s, 3, 1).start()
        x_from(s, 0, 1).wait_recv()
        x_sib(s, 1, 0).start()

    def x_end(s):
        for way in range(2):
            x_opp(s, way).wait_recv()
            x_sib(s, 2, way).start()

    def swap(i, ref):
        return remote(ref, raw.at[i, k], ws.at[i], wr.at[i], sib)

    def swap_in(i):
        return remote(raw.at[i, 1 - k], raw.at[i, 1 - k], ws.at[i], wr.at[i], sib)

    t_owner = zh * 2 + k

    def t_out(r):
        here = t_in.at[0, :, :, slice(r * PART, (r + 1) * PART)]
        return remote(here, traw.at[y], ts.at[r], tr.at[y], core_of(r, t_owner))

    def t_stays(r):
        return jnp.logical_and(t_owner == y, role == r)

    t_local = pltpu.make_async_copy(t_in.at[0, :, :, mine], traw.at[y], lsem.at[6])
    holds = zh == y // 2

    def t_from(b):
        return remote(traw.at[b], traw.at[b], ts.at[0], tr.at[b], sib)

    def t_sent():
        for r in range(2):

            @pl.when(jnp.logical_not(t_stays(r)))
            def _():
                t_out(r).wait_send()

    swap(0, w_in.at[:, other]).start()
    x_begin(0)
    swap(1, m_in.at[0, :, other]).start()
    swap(2, v_in.at[0, :, other]).start()
    for r in range(2):

        @pl.when(t_stays(r))
        def _():
            t_local.start()

        @pl.when(jnp.logical_not(t_stays(r)))
        def _():
            t_out(r).start()


    def turned(i, dst):
        for kd in range(2):
            for r in range(4):
                dst[:, kd * BLOCK + r * PART : kd * BLOCK + (r + 1) * PART] = raw[
                    i, kd, r * PART : (r + 1) * PART, :
                ].T

    locals_[0].wait()
    swap_in(0).wait_recv()
    turned(0, wt)
    ot[...] = wt[...]
    wb[...] = wt[...].astype(BF16)
    locals_[4].wait()
    locals_[5].wait()
    swap_in(1).wait_recv()
    turned(1, mt)
    swap_in(2).wait_recv()
    turned(2, vt)

    blocks = (x, xl, xr_, xo)
    order = (0, 3, 1, 2)

    def quarter(y_):
        return pl.ds(pl.multiple_of(y_ * PART, PART), PART)

    def partial_of(s, p, y_):
        b, rows = blocks[p], quarter(y_)
        return dot_nt(wb[:, :BLOCK], xg[s, b, 0, rows, :]) + dot_nt(wb[:, BLOCK:], xg[s, b, 1, rows, :])

    def y_out(s, j, p):
        return remote(ysend.at[s, j, p], yrecv.at[s, j, p], ys.at[s, j, p], yr.at[s, j, p], ydev(j))

    def z_out(s, p):
        return remote(zsend.at[s, p], zrecv.at[s, p], zs.at[s, p], zr.at[s, p], zdev)

    def g_copy(s, y_, j, p):
        here = resid.at[s, y_, p]
        return remote(here, here, gs.at[s, j, p], gr.at[s, j, p], ydev(j))

    def g_out(s, j, p):
        return g_copy(s, y, j, p)

    def g_from(s, j, p):
        return g_copy(s, (y + 4 - j) % 4, j, p)

    def forward(s, p):
        for h in range(2):
            x_sib(s, order[p], h, incoming=True).wait_recv()
        for j in (2, 1, 3):
            ysend[s, j, p] = partial_of(s, p, (y + j) % 4).astype(BF16)
            y_out(s, j, p).start()
        own[p] = partial_of(s, p, y)

    def gather_y(s, p):
        @pl.when(holds)
        def _():
            own[p] = own[p] - traw[blocks[p], s].astype(F32).T

        total = own[p]
        for j in (1, 3, 2):
            y_out(s, j, p).wait_recv()
            total = total + yrecv[s, j, p].astype(F32)
        ysum[p] = total
        zsend[s, p] = total.astype(BF16)
        z_out(s, p).start()

    def gather_z(s, p):
        z_out(s, p).wait_recv()
        resid[s, y, p] = (ysum[p] + zrecv[s, p].astype(F32)).astype(BF16)
        for j in (2, 1, 3):
            g_out(s, j, p).start()

    def rows_of(s, kd, y_, ps):
        return jnp.concatenate([xg[s, blocks[p], kd, quarter(y_), :] for p in ps], axis=0)

    def backward_own(s):
        r = jnp.concatenate([resid[s, y, p] for p in range(4)], axis=1)
        for kd in range(2):
            grad[:, kd * BLOCK : (kd + 1) * BLOCK] = dot_nn(r, rows_of(s, kd, y, range(4)))

    def backward(s):
        for ps in ((0, 1), (2, 3)):
            for j in (1, 3, 2):
                b = (y + 4 - j) % 4
                for p in ps:
                    g_from(s, j, p).wait_recv()
                r = jnp.concatenate([resid[s, b, p] for p in ps], axis=1)
                for kd in range(2):
                    grad[:, kd * BLOCK : (kd + 1) * BLOCK] += dot_nn(r, rows_of(s, kd, b, ps))

    pieces = [(h, c) for c in range(4) for h in range(2)]

    def columns(h, c):
        return slice(h * BLOCK + c * PART, h * BLOCK + (c + 1) * PART)

    def update(s, then):
        power = PRIOR + s + 1
        for h, c in pieces:
            for cut in range(2):
                part = (slice(cut * 64, cut * 64 + 64), columns(h, c))
                gradient = grad[part] * (1.0 / TOKENS)
                first = beta_first * mt[part] + (1.0 - beta_first) * gradient
                second = beta_second * vt[part] + (1.0 - beta_second) * gradient * gradient
                corrected = (
                    first
                    / (1.0 - beta_first**power)
                    / (jnp.sqrt(second / (1.0 - beta_second**power)) + epsilon_value)
                )
                old = wt[part]
                new = old - inner_rate * (corrected + decay_rate * old)
                mt[part] = first
                vt[part] = second
                wt[part] = new
                if s + 1 < STEPS:
                    wb[part] = new.astype(BF16)
            then(h, c)

    def sent(s):
        for way in range(2):
            for h in range(2):
                x_own(s, h, way).wait_send()
            x_fwd(s, way).wait_send()
        for d in range(4):
            for h in range(2):
                x_sib(s, d, h).wait_send()
        for p in range(4):
            for j in (1, 2, 3):
                y_out(s, j, p).wait_send()
                g_out(s, j, p).wait_send()
            z_out(s, p).wait_send()

    fast = g < 3
    total_steps = float(3 * STEPS + SLOW_STEPS)
    weight = jnp.where(fast, float(STEPS), float(SLOW_STEPS)) / total_steps

    def adder(h):
        return at(1 + h, y, zh)

    def slow_out(h):
        return remote(slow.at[h], slow_in, os_.at[h], or_, adder(h))

    way_in = jnp.where(g == 0, 0, 1)

    def early_out(h):
        return remote(early.at[h], early_in.at[way_in], es.at[h], er.at[way_in], adder(h))

    def early_from(i):
        return remote(early.at[0], early_in.at[i], es.at[0], er.at[i], adder(0))

    half = jnp.where(g == 2, 1, 0)
    adds = jnp.logical_or(g == 1, g == 2)

    def early_sum_out(j):
        return remote(early_sum.at[half], early_sum.at[half], as_.at[j], ar.at[half], gdev(j))

    def early_sum_from(h):
        return remote(early_sum.at[h], early_sum.at[h], as_.at[1], ar.at[h], gdev(1))

    def late_out(h, c):
        return remote(late.at[h, c], late_in.at[way_in, c], ls.at[h, c], lr.at[way_in, c], adder(h))

    def late_from(i, c):
        return remote(late.at[0, c], late_in.at[i, c], ls.at[0, c], lr.at[i, c], adder(0))

    def late_sum_out(j, c):
        return remote(late_sum.at[half, c], late_sum.at[half, c], fs.at[j, c], fr.at[half, c], gdev(j))

    def late_sum_from(h, c):
        return remote(late_sum.at[h, c], late_sum.at[h, c], fs.at[1, c], fr.at[h, c], gdev(1))

    def moved(h, c):
        return weight * (ot[:, columns(h, c)] - wt[:, columns(h, c)])

    def nothing(h, c):
        return None

    def to_slow(h, c):
        slow[h, c] = moved(h, c)

    def to_early(h, c):
        early[h, c] = moved(h, c).astype(BF16)
        if c == 3:

            @pl.when(g != 1 + h)
            def _():
                early_out(h).start()

    def to_late(h, c):
        late[h, c] = (moved(h, c) - early[h, c].astype(F32)).astype(BF16)

        @pl.when(g != 1 + h)
        def _():
            late_out(h, c).start()

    locals_[1].wait()
    forward(0, 0)
    x_middle(0)

    @pl.when(holds)
    def _():
        for b in range(4):
            stays = jnp.logical_and(b == y, k == y % 2)

            @pl.when(stays)
            def _():
                t_local.wait()

            @pl.when(jnp.logical_not(stays))
            def _():
                t_from(b).wait_recv()

    gather_y(0, 0)
    x_rest(0)
    forward(0, 1)
    forward(0, 2)

    @pl.when(fast)
    def _():
        x_begin(1)

    gather_z(0, 0)
    x_end(0)
    forward(0, 3)
    for p in (1, 2, 3):
        gather_y(0, p)

    @pl.when(fast)
    def _():
        x_middle(1)

    for p in (1, 2, 3):
        gather_z(0, p)
    backward_own(0)

    @pl.when(fast)
    def _():
        x_rest(1)

    backward(0)
    update(0, nothing)

    locals_[2].wait()
    locals_[3].wait()

    @pl.when(jnp.logical_not(fast))
    def _():
        for h, c in pieces:
            to_slow(h, c)
        for h in range(2):
            slow_out(h).start()
        sent(0)
        for i in range(3):
            swap_in(i).wait_send()
        t_sent()
        for h in range(2):
            slow_out(h).wait_send()

    @pl.when(fast)
    def _():
        for s in range(1, STEPS):
            for p in range(3):
                forward(s, p)
            x_end(s)
            if s + 1 < STEPS:
                x_begin(s + 1)
            forward(s, 3)
            sent(s - 1)
            if s == 1:
                for i in range(3):
                    swap_in(i).wait_send()
                t_sent()
            for p in range(4):
                gather_y(s, p)
            if s + 1 < STEPS:
                x_middle(s + 1)
            for p in range(4):
                gather_z(s, p)
            backward_own(s)
            if s + 1 < STEPS:
                x_rest(s + 1)
            if s + 1 == STEPS:

                @pl.when(adds)
                def _():
                    for i in range(2):
                        early_from(i).wait_recv()
                    slow_out(0).wait_recv()
                    for c in range(4):
                        total = early[half, c].astype(F32) + slow_in[c]
                        for i in range(2):
                            total = total + early_in[i, c].astype(F32)
                        rounded = total.astype(BF16)
                        early_sum[half, c] = rounded
                        left_over[c] = total - rounded.astype(F32)
                    for j in (2, 1, 3):
                        early_sum_out(j).start()

            backward(s)
            update(s, (nothing, to_early, to_late)[s])

    @pl.when(adds)
    def _():
        for c in range(4):
            total = late[half, c].astype(F32) + left_over[c]
            for i in range(2):
                late_from(i, c).wait_recv()
                total = total + late_in[i, c].astype(F32)
            late_sum[half, c] = total.astype(BF16)
            for j in (2, 1, 3):
                late_sum_out(j, c).start()

    @pl.when(fast)
    def _():
        sent(STEPS - 1)
        for h in range(2):

            @pl.when(g != 1 + h)
            def _():
                early_out(h).wait_send()
                for c in range(4):
                    late_out(h, c).wait_send()

    @pl.when(adds)
    def _():
        for j in (1, 2, 3):
            early_sum_out(j).wait_send()

    for h in range(2):

        @pl.when(g != 1 + h)
        def _():
            early_sum_from(h).wait_recv()

    def away(c):
        return remote(stage.at[1 - k, c], back.at[c], bs.at[c], br.at[c], sib)

    for c in range(4):
        for h in range(2):

            @pl.when(g != 1 + h)
            def _():
                late_sum_from(h, c).wait_recv()

            stage[h, c] = (early_sum[h, c].astype(F32) + late_sum[h, c].astype(F32)).T
        away(c).start()
    for c in range(4):
        away(c).wait_recv()
        here = slice(c * PART, (c + 1) * PART)

        @pl.when(role == 0)
        def _():
            o_ref[here, :PART] = stage[k, c]
            o_ref[here, PART:] = back[c]

        @pl.when(role == 1)
        def _():
            o_ref[here, :PART] = back[c]
            o_ref[here, PART:] = stage[k, c]

    for c in range(4):
        away(c).wait_send()

    @pl.when(adds)
    def _():
        for j in (1, 2, 3):
            for c in range(4):
                late_sum_out(j, c).wait_send()


def pseudo_of(outer_params, first_moment, second_moment, activations, targets):
    dma = pltpu.SemaphoreType.DMA
    vm = pltpu.VMEM
    hbm = pl.BlockSpec(memory_space=pltpu.HBM)
    n = STEPS
    tile = (PART, PART)
    return pl.pallas_call(
        kernel,
        out_shape=jax.ShapeDtypeStruct((512, 256), F32),
        in_specs=[hbm] * 5,
        out_specs=pl.BlockSpec(memory_space=pltpu.VMEM),
        scratch_shapes=[
            vm((n, 4, 2, 512, 512), BF16),
            vm((3, 2, 512, PART), F32),
            vm((PART, 1024), F32), vm((PART, 1024), F32), vm((PART, 1024), F32), vm((PART, 1024), F32),
            vm((PART, 1024), BF16),
            vm((4, n, *tile), BF16),
            vm((4, *tile), F32),
            vm((n, 4, 4, *tile), BF16), vm((n, 4, 4, *tile), BF16),
            vm((4, *tile), F32),
            vm((n, 4, *tile), BF16), vm((n, 4, *tile), BF16),
            vm((n, 4, 4, *tile), BF16),
            vm((PART, 1024), F32),
            vm((2, 4, *tile), F32), vm((4, *tile), F32),
            vm((2, 4, *tile), BF16), vm((2, 4, *tile), BF16), vm((2, 4, *tile), BF16),
            vm((4, *tile), F32),
            vm((2, 4, *tile), BF16), vm((2, 4, *tile), BF16), vm((2, 4, *tile), BF16),
            vm((2, 4, *tile), F32), vm((4, *tile), F32),
            dma((7,)),
            dma((n, 6)), dma((n, 6)), dma((n, 8)), dma((n, 8)),
            dma((3,)), dma((3,)), dma((2,)), dma((4,)),
            dma((n, 4, 4)), dma((n, 4, 4)), dma((n, 4)), dma((n, 4)),
            dma((n, 4, 4)), dma((n, 4, 4)),
            dma((2,)), dma, dma((2,)), dma((2,)), dma((4,)), dma((2,)),
            dma((2, 4)), dma((2, 4)), dma((4, 4)), dma((2, 4)),
            dma((4,)), dma((4,)),
        ],
        compiler_params=pltpu.CompilerParams(
            collective_id=0, has_side_effects=True, vmem_limit_bytes=63 << 20
        ),
    )(outer_params, first_moment, second_moment, activations, targets)


def local(outer_params, first_moment, second_moment, outer_moment, activations, targets):
    pseudo = pseudo_of(outer_params, first_moment, second_moment, activations, targets)
    new_moment = momentum_coef * outer_moment + pseudo
    new_params = outer_params - outer_rate * (pseudo + momentum_coef * new_moment)
    return (new_params, new_moment)


def solution(mesh):
    placed = (
        P("col", "row"),
        P("grp", "col", "row"),
        P("grp", "col", "row"),
        P("col", "row"),
        P("grp", None, "row", "col"),
        P("grp", None, "col", "row"),
    )
    return jax.shard_map(
        local,
        mesh=mesh,
        in_specs=placed,
        out_specs=(P("col", "row"), P("col", "row")),
        check_vma=False,
    )
```

```python
import functools

import jax
import jax.numpy as jnp
from jax import lax
from jax.experimental import pallas as pl
from jax.experimental.pallas import tpu as pltpu
from jax.sharding import PartitionSpec as P

TOKENS = 2048
STEPS = 3
SLOW_STEPS = 1
PRIOR = 100
BLOCK = 512
PART = 128

beta_first = 0.9
beta_second = 0.95
inner_rate = 0.01
decay_rate = 0.1
epsilon_value = 1e-08
outer_rate = 0.7
momentum_coef = 0.9

F32 = jnp.float32
BF16 = jnp.bfloat16


def dot_nt(a, b):
    return lax.dot_general(a, b, (((1,), (1,)), ((), ())), preferred_element_type=F32)


def dot_nn(a, b):
    return lax.dot_general(a, b, (((1,), (0,)), ((), ())), preferred_element_type=F32)


def kernel(
    w_in, m_in, v_in, x_in, t_in, o_ref,
    xg, raw, wt, mt, vt, ot, wb, traw, own, ysend, yrecv, ysum, zsend, zrecv, resid, grad,
    slow, slow_in, early, early_in, early_sum, left_over, late, late_in, late_sum, stage, back,
    lsem, xs, xr, ss, sr, ws, wr, ts, tr, ys, yr, zs, zr, gs, gr,
    os_, or_, es, er, as_, ar, ls, lr, fs, fr, bs, br,
):
    g = lax.axis_index("grp")
    x = lax.axis_index("row")
    col = lax.axis_index("col")
    y = col // 4
    zh = (col // 2) % 2
    k = col % 2

    def flip(g_, y_, zh_):
        return (y_ // 2 + zh_ + g_) % 2

    role = (k + flip(g, y, zh)) % 2

    def at(g_, y_, zh_):
        return {"grp": g_, "col": y_ * 4 + zh_ * 2 + (role + flip(g_, y_, zh_)) % 2}

    sib = {"col": y * 4 + zh * 2 + (1 - k)}
    zdev = at(g, y, 1 - zh)
    across = y * 4 + zh * 2 + (1 - k)
    right = {"row": (x + 1) % 4, "col": across}
    left = {"row": (x + 3) % 4, "col": across}
    xl, xr_, xo = (x + 3) % 4, (x + 1) % 4, (x + 2) % 4

    def ydev(j):
        return at(g, (y + j) % 4, zh)

    def core_of(role_, y_):
        return {"col": y_ * 4 + zh * 2 + (role_ + flip(g, y_, zh)) % 2}

    def gdev(j):
        return at((g + j) % 4, y, zh)

    def remote(src, dst, s_sem, r_sem, dev):
        return pltpu.make_async_remote_copy(
            src_ref=src, dst_ref=dst, send_sem=s_sem, recv_sem=r_sem,
            device_id=dev, device_id_type=pl.DeviceIdType.MESH,
        )

    barrier = pltpu.get_barrier_semaphore()
    peers = [sib, right, left, zdev] + [ydev(j) for j in (1, 2, 3)] + [gdev(j) for j in (1, 2, 3)]
    peers += [core_of(1 - role, (y + j) % 4) for j in (1, 2, 3)]
    for dev in peers:
        pl.semaphore_signal(barrier, inc=1, device_id=dev, device_id_type=pl.DeviceIdType.MESH)

    mine = pl.ds(pl.multiple_of(role * PART, PART), PART)
    other = pl.ds(pl.multiple_of((1 - role) * PART, PART), PART)
    locals_ = [pltpu.make_async_copy(w_in.at[:, mine], raw.at[0, k], lsem.at[0])]
    locals_ += [pltpu.make_async_copy(x_in.at[0, s], xg.at[s, x, k], lsem.at[1 + s]) for s in range(STEPS)]
    locals_ += [pltpu.make_async_copy(m_in.at[0, :, mine], raw.at[1, k], lsem.at[4])]
    locals_ += [pltpu.make_async_copy(v_in.at[0, :, mine], raw.at[2, k], lsem.at[5])]
    for c in locals_:
        c.start()

    pl.semaphore_wait(barrier, len(peers))

    halves = (pl.ds(0, 256), pl.ds(256, 256))

    def x_copy(s, slot, src, dst, way):
        return remote(src, dst, xs.at[s, slot], xr.at[s, slot], (right, left)[way])

    def x_own(s, h, way):
        return x_copy(s, 2 * way + h, x_in.at[0, s, halves[h]], xg.at[s, x, k, halves[h]], way)

    def x_from(s, h, way):
        here = xg.at[s, (xl, xr_)[way], 1 - k, halves[h]]
        return x_copy(s, 2 * way + h, here, here, way)

    def x_fwd(s, way):
        here = xg.at[s, (xl, xr_)[way], 1 - k, halves[way]]
        return x_copy(s, 4 + way, here, here, way)

    def x_opp(s, way):
        here = xg.at[s, xo, k, halves[way]]
        return x_copy(s, 4 + way, here, here, way)

    def x_sib(s, d, h, src=None, incoming=False):
        kd = (k + d + incoming) % 2
        here = xg.at[s, (x + d) % 4, kd, halves[h]]
        return remote(here if src is None else src, here, ss.at[s, 2 * d + h], sr.at[s, 2 * d + h], sib)

    def x_begin(s):
        x_own(s, 0, 0).start()
        x_own(s, 1, 1).start()
        x_own(s, 1, 0).start()
        x_own(s, 0, 1).start()
        for h in range(2):
            x_sib(s, 0, h, x_in.at[0, s, halves[h]]).start()

    def x_middle(s):
        x_from(s, 0, 0).wait_recv()
        x_fwd(s, 0).start()
        x_sib(s, 3, 0).start()
        x_from(s, 1, 1).wait_recv()
        x_fwd(s, 1).start()
        x_sib(s, 1, 1).start()

    def x_rest(s):
        x_from(s, 1, 0).wait_recv()
        x_sib(s, 3, 1).start()
        x_from(s, 0, 1).wait_recv()
        x_sib(s, 1, 0).start()

    def x_end(s):
        for way in range(2):
            x_opp(s, way).wait_recv()
            x_sib(s, 2, way).start()

    def swap(i, ref):
        return remote(ref, raw.at[i, k], ws.at[i], wr.at[i], sib)

    def swap_in(i):
        return remote(raw.at[i, 1 - k], raw.at[i, 1 - k], ws.at[i], wr.at[i], sib)

    t_owner = zh * 2 + k

    def t_out(r):
        here = t_in.at[0, :, :, slice(r * PART, (r + 1) * PART)]
        return remote(here, traw.at[y], ts.at[r], tr.at[y], core_of(r, t_owner))

    def t_stays(r):
        return jnp.logical_and(t_owner == y, role == r)

    t_local = pltpu.make_async_copy(t_in.at[0, :, :, mine], traw.at[y], lsem.at[6])
    holds = zh == y // 2

    def t_from(b):
        return remote(traw.at[b], traw.at[b], ts.at[0], tr.at[b], sib)

    def t_sent():
        for r in range(2):

            @pl.when(jnp.logical_not(t_stays(r)))
            def _():
                t_out(r).wait_send()

    swap(0, w_in.at[:, other]).start()
    x_begin(0)
    swap(1, m_in.at[0, :, other]).start()
    swap(2, v_in.at[0, :, other]).start()
    for r in range(2):

        @pl.when(t_stays(r))
        def _():
            t_local.start()

        @pl.when(jnp.logical_not(t_stays(r)))
        def _():
            t_out(r).start()


    def turned(i, dst):
        for kd in range(2):
            for r in range(4):
                dst[:, kd * BLOCK + r * PART : kd * BLOCK + (r + 1) * PART] = raw[
                    i, kd, r * PART : (r + 1) * PART, :
                ].T

    locals_[0].wait()
    swap_in(0).wait_recv()
    turned(0, wt)
    ot[...] = wt[...]
    wb[...] = wt[...].astype(BF16)
    locals_[4].wait()
    locals_[5].wait()
    swap_in(1).wait_recv()
    turned(1, mt)
    swap_in(2).wait_recv()
    turned(2, vt)

    blocks = (x, xl, xr_, xo)
    order = (0, 3, 1, 2)

    def quarter(y_):
        return pl.ds(pl.multiple_of(y_ * PART, PART), PART)

    def partial_of(s, p, y_):
        b, rows = blocks[p], quarter(y_)
        return dot_nt(wb[:, :BLOCK], xg[s, b, 0, rows, :]) + dot_nt(wb[:, BLOCK:], xg[s, b, 1, rows, :])

    def y_out(s, j, p):
        return remote(ysend.at[s, j, p], yrecv.at[s, j, p], ys.at[s, j, p], yr.at[s, j, p], ydev(j))

    def z_out(s, p):
        return remote(zsend.at[s, p], zrecv.at[s, p], zs.at[s, p], zr.at[s, p], zdev)

    def g_copy(s, y_, j, p):
        here = resid.at[s, y_, p]
        return remote(here, here, gs.at[s, j, p], gr.at[s, j, p], ydev(j))

    def g_out(s, j, p):
        return g_copy(s, y, j, p)

    def g_from(s, j, p):
        return g_copy(s, (y + 4 - j) % 4, j, p)

    def forward(s, p):
        for h in range(2):
            x_sib(s, order[p], h, incoming=True).wait_recv()
        for j in (2, 1, 3):
            ysend[s, j, p] = partial_of(s, p, (y + j) % 4).astype(BF16)
            y_out(s, j, p).start()
        own[p] = partial_of(s, p, y)

    def gather_y(s, p):
        @pl.when(holds)
        def _():
            own[p] = own[p] - traw[blocks[p], s].astype(F32).T

        total = own[p]
        for j in (1, 3, 2):
            y_out(s, j, p).wait_recv()
            total = total + yrecv[s, j, p].astype(F32)
        ysum[p] = total
        zsend[s, p] = total.astype(BF16)
        z_out(s, p).start()

    def gather_z(s, p):
        z_out(s, p).wait_recv()
        resid[s, y, p] = (ysum[p] + zrecv[s, p].astype(F32)).astype(BF16)
        for j in (2, 1, 3):
            g_out(s, j, p).start()

    def rows_of(s, kd, y_, ps):
        return jnp.concatenate([xg[s, blocks[p], kd, quarter(y_), :] for p in ps], axis=0)

    def backward_own(s):
        r = jnp.concatenate([resid[s, y, p] for p in range(4)], axis=1)
        for kd in range(2):
            grad[:, kd * BLOCK : (kd + 1) * BLOCK] = dot_nn(r, rows_of(s, kd, y, range(4)))

    def backward(s):
        for ps in ((0, 1), (2, 3)):
            for j in (1, 3, 2):
                b = (y + 4 - j) % 4
                for p in ps:
                    g_from(s, j, p).wait_recv()
                r = jnp.concatenate([resid[s, b, p] for p in ps], axis=1)
                for kd in range(2):
                    grad[:, kd * BLOCK : (kd + 1) * BLOCK] += dot_nn(r, rows_of(s, kd, b, ps))

    pieces = [(h, c) for c in range(4) for h in range(2)]

    def columns(h, c):
        return slice(h * BLOCK + c * PART, h * BLOCK + (c + 1) * PART)

    def update(s, then):
        power = PRIOR + s + 1
        for h, c in pieces:
            for cut in range(2):
                part = (slice(cut * 64, cut * 64 + 64), columns(h, c))
                gradient = grad[part] * (1.0 / TOKENS)
                first = beta_first * mt[part] + (1.0 - beta_first) * gradient
                second = beta_second * vt[part] + (1.0 - beta_second) * gradient * gradient
                corrected = (
                    first
                    / (1.0 - beta_first**power)
                    / (jnp.sqrt(second / (1.0 - beta_second**power)) + epsilon_value)
                )
                old = wt[part]
                new = old - inner_rate * (corrected + decay_rate * old)
                mt[part] = first
                vt[part] = second
                wt[part] = new
                if s + 1 < STEPS:
                    wb[part] = new.astype(BF16)
            then(h, c)

    def sent(s):
        for way in range(2):
            for h in range(2):
                x_own(s, h, way).wait_send()
            x_fwd(s, way).wait_send()
        for d in range(4):
            for h in range(2):
                x_sib(s, d, h).wait_send()
        for p in range(4):
            for j in (1, 2, 3):
                y_out(s, j, p).wait_send()
                g_out(s, j, p).wait_send()
            z_out(s, p).wait_send()

    fast = g < 3
    total_steps = float(3 * STEPS + SLOW_STEPS)
    weight = jnp.where(fast, float(STEPS), float(SLOW_STEPS)) / total_steps

    def adder(h):
        return at(1 + h, y, zh)

    def slow_out(h):
        return remote(slow.at[h], slow_in, os_.at[h], or_, adder(h))

    way_in = jnp.where(g == 0, 0, 1)

    def early_out(h):
        return remote(early.at[h], early_in.at[way_in], es.at[h], er.at[way_in], adder(h))

    def early_from(i):
        return remote(early.at[0], early_in.at[i], es.at[0], er.at[i], adder(0))

    half = jnp.where(g == 2, 1, 0)
    adds = jnp.logical_or(g == 1, g == 2)

    def early_sum_out(j):
        return remote(early_sum.at[half], early_sum.at[half], as_.at[j], ar.at[half], gdev(j))

    def early_sum_from(h):
        return remote(early_sum.at[h], early_sum.at[h], as_.at[1], ar.at[h], gdev(1))

    def late_out(h, c):
        return remote(late.at[h, c], late_in.at[way_in, c], ls.at[h, c], lr.at[way_in, c], adder(h))

    def late_from(i, c):
        return remote(late.at[0, c], late_in.at[i, c], ls.at[0, c], lr.at[i, c], adder(0))

    def late_sum_out(j, c):
        return remote(late_sum.at[half, c], late_sum.at[half, c], fs.at[j, c], fr.at[half, c], gdev(j))

    def late_sum_from(h, c):
        return remote(late_sum.at[h, c], late_sum.at[h, c], fs.at[1, c], fr.at[h, c], gdev(1))

    def moved(h, c):
        return weight * (ot[:, columns(h, c)] - wt[:, columns(h, c)])

    def nothing(h, c):
        return None

    def to_slow(h, c):
        slow[h, c] = moved(h, c)

    def to_early(h, c):
        early[h, c] = moved(h, c).astype(BF16)
        if c == 3:

            @pl.when(g != 1 + h)
            def _():
                early_out(h).start()

    def to_late(h, c):
        late[h, c] = (moved(h, c) - early[h, c].astype(F32)).astype(BF16)

        @pl.when(g != 1 + h)
        def _():
            late_out(h, c).start()

    locals_[1].wait()
    forward(0, 0)
    x_middle(0)

    @pl.when(holds)
    def _():
        for b in range(4):
            stays = jnp.logical_and(b == y, k == y % 2)

            @pl.when(stays)
            def _():
                t_local.wait()

            @pl.when(jnp.logical_not(stays))
            def _():
                t_from(b).wait_recv()

    gather_y(0, 0)
    x_rest(0)
    forward(0, 1)
    forward(0, 2)

    @pl.when(fast)
    def _():
        x_begin(1)

    gather_z(0, 0)
    x_end(0)
    forward(0, 3)
    for p in (1, 2, 3):
        gather_y(0, p)

    @pl.when(fast)
    def _():
        x_middle(1)

    for p in (1, 2, 3):
        gather_z(0, p)
    backward_own(0)

    @pl.when(fast)
    def _():
        x_rest(1)

    backward(0)
    update(0, nothing)

    locals_[2].wait()
    locals_[3].wait()

    @pl.when(jnp.logical_not(fast))
    def _():
        for h, c in pieces:
            to_slow(h, c)
        for h in range(2):
            slow_out(h).start()
        sent(0)
        for i in range(3):
            swap_in(i).wait_send()
        t_sent()
        for h in range(2):
            slow_out(h).wait_send()

    @pl.when(fast)
    def _():
        for s in range(1, STEPS):
            for p in range(3):
                forward(s, p)
            x_end(s)
            if s + 1 < STEPS:
                x_begin(s + 1)
            forward(s, 3)
            sent(s - 1)
            if s == 1:
                for i in range(3):
                    swap_in(i).wait_send()
                t_sent()
            for p in range(4):
                gather_y(s, p)
            if s + 1 < STEPS:
                x_middle(s + 1)
            for p in range(4):
                gather_z(s, p)
            backward_own(s)
            if s + 1 < STEPS:
                x_rest(s + 1)
            if s + 1 == STEPS:

                @pl.when(adds)
                def _():
                    for i in range(2):
                        early_from(i).wait_recv()
                    slow_out(0).wait_recv()
                    for c in range(4):
                        total = early[half, c].astype(F32) + slow_in[c]
                        for i in range(2):
                            total = total + early_in[i, c].astype(F32)
                        rounded = total.astype(BF16)
                        early_sum[half, c] = rounded
                        left_over[c] = total - rounded.astype(F32)
                    for j in (2, 1, 3):
                        early_sum_out(j).start()

            backward(s)
            update(s, (nothing, to_early, to_late)[s])

    @pl.when(adds)
    def _():
        for c in range(4):
            total = late[half, c].astype(F32) + left_over[c]
            for i in range(2):
                late_from(i, c).wait_recv()
                total = total + late_in[i, c].astype(F32)
            late_sum[half, c] = total.astype(BF16)
            for j in (2, 1, 3):
                late_sum_out(j, c).start()

    @pl.when(fast)
    def _():
        sent(STEPS - 1)
        for h in range(2):

            @pl.when(g != 1 + h)
            def _():
                early_out(h).wait_send()
                for c in range(4):
                    late_out(h, c).wait_send()

    @pl.when(adds)
    def _():
        for j in (1, 2, 3):
            early_sum_out(j).wait_send()

    for h in range(2):

        @pl.when(g != 1 + h)
        def _():
            early_sum_from(h).wait_recv()

    def away(c):
        return remote(stage.at[1 - k, c], back.at[c], bs.at[c], br.at[c], sib)

    for c in range(4):
        for h in range(2):

            @pl.when(g != 1 + h)
            def _():
                late_sum_from(h, c).wait_recv()

            stage[h, c] = (early_sum[h, c].astype(F32) + late_sum[h, c].astype(F32)).T
        away(c).start()
    for c in range(4):
        away(c).wait_recv()
        here = slice(c * PART, (c + 1) * PART)

        @pl.when(role == 0)
        def _():
            o_ref[here, :PART] = stage[k, c]
            o_ref[here, PART:] = back[c]

        @pl.when(role == 1)
        def _():
            o_ref[here, :PART] = back[c]
            o_ref[here, PART:] = stage[k, c]

    for c in range(4):
        away(c).wait_send()

    @pl.when(adds)
    def _():
        for j in (1, 2, 3):
            for c in range(4):
                late_sum_out(j, c).wait_send()


def pseudo_of(outer_params, first_moment, second_moment, activations, targets):
    dma = pltpu.SemaphoreType.DMA
    vm = pltpu.VMEM
    hbm = pl.BlockSpec(memory_space=pltpu.HBM)
    n = STEPS
    tile = (PART, PART)
    return pl.pallas_call(
        kernel,
        out_shape=jax.ShapeDtypeStruct((512, 256), F32),
        in_specs=[hbm] * 5,
        out_specs=pl.BlockSpec(memory_space=pltpu.VMEM),
        scratch_shapes=[
            vm((n, 4, 2, 512, 512), BF16),
            vm((3, 2, 512, PART), F32),
            vm((PART, 1024), F32), vm((PART, 1024), F32), vm((PART, 1024), F32), vm((PART, 1024), F32),
            vm((PART, 1024), BF16),
            vm((4, n, *tile), BF16),
            vm((4, *tile), F32),
            vm((n, 4, 4, *tile), BF16), vm((n, 4, 4, *tile), BF16),
            vm((4, *tile), F32),
            vm((n, 4, *tile), BF16), vm((n, 4, *tile), BF16),
            vm((n, 4, 4, *tile), BF16),
            vm((PART, 1024), F32),
            vm((2, 4, *tile), F32), vm((4, *tile), F32),
            vm((2, 4, *tile), BF16), vm((2, 4, *tile), BF16), vm((2, 4, *tile), BF16),
            vm((4, *tile), F32),
            vm((2, 4, *tile), BF16), vm((2, 4, *tile), BF16), vm((2, 4, *tile), BF16),
            vm((2, 4, *tile), F32), vm((4, *tile), F32),
            dma((7,)),
            dma((n, 6)), dma((n, 6)), dma((n, 8)), dma((n, 8)),
            dma((3,)), dma((3,)), dma((2,)), dma((4,)),
            dma((n, 4, 4)), dma((n, 4, 4)), dma((n, 4)), dma((n, 4)),
            dma((n, 4, 4)), dma((n, 4, 4)),
            dma((2,)), dma, dma((2,)), dma((2,)), dma((4,)), dma((2,)),
            dma((2, 4)), dma((2, 4)), dma((4, 4)), dma((2, 4)),
            dma((4,)), dma((4,)),
        ],
        compiler_params=pltpu.CompilerParams(
            collective_id=0, has_side_effects=True, vmem_limit_bytes=48 << 20
        ),
    )(*[pltpu.with_memory_space_constraint(a, pltpu.HBM) for a in (outer_params, first_moment, second_moment, activations, targets)])


def local(outer_params, first_moment, second_moment, outer_moment, activations, targets):
    pseudo = pseudo_of(outer_params, first_moment, second_moment, activations, targets)
    new_moment = momentum_coef * outer_moment + pseudo
    new_params = outer_params - outer_rate * (pseudo + momentum_coef * new_moment)
    return (new_params, new_moment)


def solution(mesh):
    placed = (
        P("col", "row"),
        P("grp", "col", "row"),
        P("grp", "col", "row"),
        P("col", "row"),
        P("grp", None, "row", "col"),
        P("grp", None, "col", "row"),
    )
    return jax.shard_map(
        local,
        mesh=mesh,
        in_specs=placed,
        out_specs=(P("col", "row"), P("col", "row")),
        check_vma=False,
    )
```

```python
import functools

import jax
import jax.numpy as jnp
from jax import lax
from jax.experimental import pallas as pl
from jax.experimental.pallas import tpu as pltpu
from jax.sharding import PartitionSpec as P

TOKENS = 2048
STEPS = 3
SLOW_STEPS = 1
PRIOR = 100
BLOCK = 512
PART = 128

beta_first = 0.9
beta_second = 0.95
inner_rate = 0.01
decay_rate = 0.1
epsilon_value = 1e-08
outer_rate = 0.7
momentum_coef = 0.9

F32 = jnp.float32
BF16 = jnp.bfloat16


def dot_nt(a, b):
    return lax.dot_general(a, b, (((1,), (1,)), ((), ())), preferred_element_type=F32)


def dot_nn(a, b):
    return lax.dot_general(a, b, (((1,), (0,)), ((), ())), preferred_element_type=F32)


def kernel(
    w_in, m_in, v_in, x_in, t_in, o_ref,
    xg, raw, wt, mt, vt, ot, wb, traw, own, ysend, yrecv, ysum, zsend, zrecv, resid, grad,
    slow, slow_in, early, early_in, early_sum, left_over, late, late_in, late_sum, stage, back,
    lsem, xs, xr, ss, sr, ws, wr, ts, tr, ys, yr, zs, zr, gs, gr,
    os_, or_, es, er, as_, ar, ls, lr, fs, fr, bs, br,
):
    g = lax.axis_index("grp")
    x = lax.axis_index("row")
    col = lax.axis_index("col")
    y = col // 4
    zh = (col // 2) % 2
    k = col % 2

    def flip(g_, y_, zh_):
        return (y_ // 2 + zh_ + g_) % 2

    role = (k + flip(g, y, zh)) % 2

    def at(g_, y_, zh_):
        return {"grp": g_, "col": y_ * 4 + zh_ * 2 + (role + flip(g_, y_, zh_)) % 2}

    sib = {"col": y * 4 + zh * 2 + (1 - k)}
    zdev = at(g, y, 1 - zh)
    across = y * 4 + zh * 2 + (1 - k)
    right = {"row": (x + 1) % 4, "col": across}
    left = {"row": (x + 3) % 4, "col": across}
    xl, xr_, xo = (x + 3) % 4, (x + 1) % 4, (x + 2) % 4

    def ydev(j):
        return at(g, (y + j) % 4, zh)

    def core_of(role_, y_):
        return {"col": y_ * 4 + zh * 2 + (role_ + flip(g, y_, zh)) % 2}

    def gdev(j):
        return at((g + j) % 4, y, zh)

    def remote(src, dst, s_sem, r_sem, dev):
        return pltpu.make_async_remote_copy(
            src_ref=src, dst_ref=dst, send_sem=s_sem, recv_sem=r_sem,
            device_id=dev, device_id_type=pl.DeviceIdType.MESH,
        )

    barrier = pltpu.get_barrier_semaphore()
    peers = [sib, right, left, zdev] + [ydev(j) for j in (1, 2, 3)] + [gdev(j) for j in (1, 2, 3)]
    peers += [core_of(1 - role, (y + j) % 4) for j in (1, 2, 3)]
    for dev in peers:
        pl.semaphore_signal(barrier, inc=1, device_id=dev, device_id_type=pl.DeviceIdType.MESH)

    mine = pl.ds(pl.multiple_of(role * PART, PART), PART)
    other = pl.ds(pl.multiple_of((1 - role) * PART, PART), PART)
    locals_ = [pltpu.make_async_copy(w_in.at[:, mine], raw.at[0, k], lsem.at[0])]
    locals_ += [pltpu.make_async_copy(x_in.at[0, s], xg.at[s, x, k], lsem.at[1 + s]) for s in range(STEPS)]
    locals_ += [pltpu.make_async_copy(m_in.at[0, :, mine], raw.at[1, k], lsem.at[4])]
    locals_ += [pltpu.make_async_copy(v_in.at[0, :, mine], raw.at[2, k], lsem.at[5])]
    for c in locals_:
        c.start()

    pl.semaphore_wait(barrier, len(peers))

    halves = (pl.ds(0, 256), pl.ds(256, 256))

    def x_copy(s, slot, src, dst, way):
        return remote(src, dst, xs.at[s, slot], xr.at[s, slot], (right, left)[way])

    def x_own(s, h, way):
        return x_copy(s, 2 * way + h, x_in.at[0, s, halves[h]], xg.at[s, x, k, halves[h]], way)

    def x_from(s, h, way):
        here = xg.at[s, (xl, xr_)[way], 1 - k, halves[h]]
        return x_copy(s, 2 * way + h, here, here, way)

    def x_fwd(s, way):
        here = xg.at[s, (xl, xr_)[way], 1 - k, halves[way]]
        return x_copy(s, 4 + way, here, here, way)

    def x_opp(s, way):
        here = xg.at[s, xo, k, halves[way]]
        return x_copy(s, 4 + way, here, here, way)

    def x_sib(s, d, h, src=None, incoming=False):
        kd = (k + d + incoming) % 2
        here = xg.at[s, (x + d) % 4, kd, halves[h]]
        return remote(here if src is None else src, here, ss.at[s, 2 * d + h], sr.at[s, 2 * d + h], sib)

    def x_begin(s):
        x_own(s, 0, 0).start()
        x_own(s, 1, 1).start()
        x_own(s, 1, 0).start()
        x_own(s, 0, 1).start()
        for h in range(2):
            x_sib(s, 0, h, x_in.at[0, s, halves[h]]).start()

    def x_middle(s):
        x_from(s, 0, 0).wait_recv()
        x_fwd(s, 0).start()
        x_sib(s, 3, 0).start()
        x_from(s, 1, 1).wait_recv()
        x_fwd(s, 1).start()
        x_sib(s, 1, 1).start()

    def x_rest(s):
        x_from(s, 1, 0).wait_recv()
        x_sib(s, 3, 1).start()
        x_from(s, 0, 1).wait_recv()
        x_sib(s, 1, 0).start()

    def x_end(s):
        for way in range(2):
            x_opp(s, way).wait_recv()
            x_sib(s, 2, way).start()

    def swap(i, ref):
        return remote(ref, raw.at[i, k], ws.at[i], wr.at[i], sib)

    def swap_in(i):
        return remote(raw.at[i, 1 - k], raw.at[i, 1 - k], ws.at[i], wr.at[i], sib)

    t_owner = zh * 2 + k

    def t_out(r):
        here = t_in.at[0, :, :, slice(r * PART, (r + 1) * PART)]
        return remote(here, traw.at[y], ts.at[r], tr.at[y], core_of(r, t_owner))

    def t_stays(r):
        return jnp.logical_and(t_owner == y, role == r)

    t_local = pltpu.make_async_copy(t_in.at[0, :, :, mine], traw.at[y], lsem.at[6])
    holds = zh == y // 2

    def t_from(b):
        return remote(traw.at[b], traw.at[b], ts.at[0], tr.at[b], sib)

    def t_sent():
        for r in range(2):

            @pl.when(jnp.logical_not(t_stays(r)))
            def _():
                t_out(r).wait_send()

    swap(0, w_in.at[:, other]).start()
    x_begin(0)
    swap(1, m_in.at[0, :, other]).start()
    swap(2, v_in.at[0, :, other]).start()
    for r in range(2):

        @pl.when(t_stays(r))
        def _():
            t_local.start()

        @pl.when(jnp.logical_not(t_stays(r)))
        def _():
            t_out(r).start()


    def turned(i, dst):
        for kd in range(2):
            for r in range(4):
                dst[:, kd * BLOCK + r * PART : kd * BLOCK + (r + 1) * PART] = raw[
                    i, kd, r * PART : (r + 1) * PART, :
                ].T

    locals_[0].wait()
    swap_in(0).wait_recv()
    turned(0, wt)
    ot[...] = wt[...]
    wb[...] = wt[...].astype(BF16)
    locals_[4].wait()
    locals_[5].wait()
    swap_in(1).wait_recv()
    turned(1, mt)
    swap_in(2).wait_recv()
    turned(2, vt)

    blocks = (x, xl, xr_, xo)
    order = (0, 3, 1, 2)

    def quarter(y_):
        return pl.ds(pl.multiple_of(y_ * PART, PART), PART)

    def partial_of(s, p, y_):
        b, rows = blocks[p], quarter(y_)
        return dot_nt(wb[:, :BLOCK], xg[s, b, 0, rows, :]) + dot_nt(wb[:, BLOCK:], xg[s, b, 1, rows, :])

    def y_out(s, j, p):
        return remote(ysend.at[s, j, p], yrecv.at[s, j, p], ys.at[s, j, p], yr.at[s, j, p], ydev(j))

    def z_out(s, p):
        return remote(zsend.at[s, p], zrecv.at[s, p], zs.at[s, p], zr.at[s, p], zdev)

    def g_copy(s, y_, j, p):
        here = resid.at[s, y_, p]
        return remote(here, here, gs.at[s, j, p], gr.at[s, j, p], ydev(j))

    def g_out(s, j, p):
        return g_copy(s, y, j, p)

    def g_from(s, j, p):
        return g_copy(s, (y + 4 - j) % 4, j, p)

    def forward(s, p):
        for h in range(2):
            x_sib(s, order[p], h, incoming=True).wait_recv()
        for j in (2, 1, 3):
            ysend[s, j, p] = partial_of(s, p, (y + j) % 4).astype(BF16)
            y_out(s, j, p).start()
        own[p] = partial_of(s, p, y)

    def gather_y(s, p):
        @pl.when(holds)
        def _():
            own[p] = own[p] - traw[blocks[p], s].astype(F32).T

        total = own[p]
        for j in (1, 3, 2):
            y_out(s, j, p).wait_recv()
            total = total + yrecv[s, j, p].astype(F32)
        ysum[p] = total
        zsend[s, p] = total.astype(BF16)
        z_out(s, p).start()

    def gather_z(s, p):
        z_out(s, p).wait_recv()
        resid[s, y, p] = (ysum[p] + zrecv[s, p].astype(F32)).astype(BF16)
        for j in (2, 1, 3):
            g_out(s, j, p).start()

    def rows_of(s, kd, y_, ps):
        return jnp.concatenate([xg[s, blocks[p], kd, quarter(y_), :] for p in ps], axis=0)

    def backward_own(s):
        r = jnp.concatenate([resid[s, y, p] for p in range(4)], axis=1)
        for kd in range(2):
            grad[:, kd * BLOCK : (kd + 1) * BLOCK] = dot_nn(r, rows_of(s, kd, y, range(4)))

    def backward(s):
        for ps in ((0, 1), (2, 3)):
            for j in (1, 3, 2):
                b = (y + 4 - j) % 4
                for p in ps:
                    g_from(s, j, p).wait_recv()
                r = jnp.concatenate([resid[s, b, p] for p in ps], axis=1)
                for kd in range(2):
                    grad[:, kd * BLOCK : (kd + 1) * BLOCK] += dot_nn(r, rows_of(s, kd, b, ps))

    pieces = [(h, c) for c in range(4) for h in range(2)]

    def columns(h, c):
        return slice(h * BLOCK + c * PART, h * BLOCK + (c + 1) * PART)

    def update(s, then):
        power = PRIOR + s + 1
        for h, c in pieces:
            for cut in range(2):
                part = (slice(cut * 64, cut * 64 + 64), columns(h, c))
                gradient = grad[part] * (1.0 / TOKENS)
                first = beta_first * mt[part] + (1.0 - beta_first) * gradient
                second = beta_second * vt[part] + (1.0 - beta_second) * gradient * gradient
                corrected = (
                    first
                    / (1.0 - beta_first**power)
                    / (jnp.sqrt(second / (1.0 - beta_second**power)) + epsilon_value)
                )
                old = wt[part]
                new = old - inner_rate * (corrected + decay_rate * old)
                mt[part] = first
                vt[part] = second
                wt[part] = new
                if s + 1 < STEPS:
                    wb[part] = new.astype(BF16)
            then(h, c)

    def sent(s):
        for way in range(2):
            for h in range(2):
                x_own(s, h, way).wait_send()
            x_fwd(s, way).wait_send()
        for d in range(4):
            for h in range(2):
                x_sib(s, d, h).wait_send()
        for p in range(4):
            for j in (1, 2, 3):
                y_out(s, j, p).wait_send()
                g_out(s, j, p).wait_send()
            z_out(s, p).wait_send()

    fast = g < 3
    total_steps = float(3 * STEPS + SLOW_STEPS)
    weight = jnp.where(fast, float(STEPS), float(SLOW_STEPS)) / total_steps

    def adder(h):
        return at(1 + h, y, zh)

    def slow_out(h):
        return remote(slow.at[h], slow_in, os_.at[h], or_, adder(h))

    way_in = jnp.where(g == 0, 0, 1)

    def early_out(h):
        return remote(early.at[h], early_in.at[way_in], es.at[h], er.at[way_in], adder(h))

    def early_from(i):
        return remote(early.at[0], early_in.at[i], es.at[0], er.at[i], adder(0))

    half = jnp.where(g == 2, 1, 0)
    adds = jnp.logical_or(g == 1, g == 2)

    def early_sum_out(j):
        return remote(early_sum.at[half], early_sum.at[half], as_.at[j], ar.at[half], gdev(j))

    def early_sum_from(h):
        return remote(early_sum.at[h], early_sum.at[h], as_.at[1], ar.at[h], gdev(1))

    def late_out(h, c):
        return remote(late.at[h, c], late_in.at[way_in, c], ls.at[h, c], lr.at[way_in, c], adder(h))

    def late_from(i, c):
        return remote(late.at[0, c], late_in.at[i, c], ls.at[0, c], lr.at[i, c], adder(0))

    def late_sum_out(j, c):
        return remote(late_sum.at[half, c], late_sum.at[half, c], fs.at[j, c], fr.at[half, c], gdev(j))

    def late_sum_from(h, c):
        return remote(late_sum.at[h, c], late_sum.at[h, c], fs.at[1, c], fr.at[h, c], gdev(1))

    def moved(h, c):
        return weight * (ot[:, columns(h, c)] - wt[:, columns(h, c)])

    def nothing(h, c):
        return None

    def to_slow(h, c):
        slow[h, c] = moved(h, c)

    def to_early(h, c):
        early[h, c] = moved(h, c).astype(BF16)
        if c == 3:

            @pl.when(g != 1 + h)
            def _():
                early_out(h).start()

    def to_late(h, c):
        late[h, c] = (moved(h, c) - early[h, c].astype(F32)).astype(BF16)

        @pl.when(g != 1 + h)
        def _():
            late_out(h, c).start()

    locals_[1].wait()
    forward(0, 0)
    x_middle(0)

    @pl.when(holds)
    def _():
        for b in range(4):
            stays = jnp.logical_and(b == y, k == y % 2)

            @pl.when(stays)
            def _():
                t_local.wait()

            @pl.when(jnp.logical_not(stays))
            def _():
                t_from(b).wait_recv()

    gather_y(0, 0)
    x_rest(0)
    forward(0, 1)
    forward(0, 2)

    @pl.when(fast)
    def _():
        x_begin(1)

    gather_z(0, 0)
    x_end(0)
    forward(0, 3)
    for p in (1, 2, 3):
        gather_y(0, p)

    @pl.when(fast)
    def _():
        x_middle(1)

    for p in (1, 2, 3):
        gather_z(0, p)
    backward_own(0)

    @pl.when(fast)
    def _():
        x_rest(1)
        x_begin(2)

    backward(0)
    update(0, nothing)

    locals_[2].wait()
    locals_[3].wait()

    @pl.when(jnp.logical_not(fast))
    def _():
        for h, c in pieces:
            to_slow(h, c)
        for h in range(2):
            slow_out(h).start()
        sent(0)
        for i in range(3):
            swap_in(i).wait_send()
        t_sent()
        for h in range(2):
            slow_out(h).wait_send()

    @pl.when(fast)
    def _():
        for s in range(1, STEPS):
            for p in range(3):
                forward(s, p)
            x_end(s)
            forward(s, 3)
            sent(s - 1)
            if s == 1:
                for i in range(3):
                    swap_in(i).wait_send()
                t_sent()
            for p in range(4):
                gather_y(s, p)
            if s + 1 < STEPS:
                x_middle(s + 1)
            for p in range(4):
                gather_z(s, p)
            backward_own(s)
            if s + 1 < STEPS:
                x_rest(s + 1)
            if s + 1 == STEPS:

                @pl.when(adds)
                def _():
                    for i in range(2):
                        early_from(i).wait_recv()
                    slow_out(0).wait_recv()
                    for c in range(4):
                        total = early[half, c].astype(F32) + slow_in[c]
                        for i in range(2):
                            total = total + early_in[i, c].astype(F32)
                        rounded = total.astype(BF16)
                        early_sum[half, c] = rounded
                        left_over[c] = total - rounded.astype(F32)
                    for j in (2, 1, 3):
                        early_sum_out(j).start()

            backward(s)
            update(s, (nothing, to_early, to_late)[s])

    @pl.when(adds)
    def _():
        for c in range(4):
            total = late[half, c].astype(F32) + left_over[c]
            for i in range(2):
                late_from(i, c).wait_recv()
                total = total + late_in[i, c].astype(F32)
            late_sum[half, c] = total.astype(BF16)
            for j in (2, 1, 3):
                late_sum_out(j, c).start()

    @pl.when(fast)
    def _():
        sent(STEPS - 1)
        for h in range(2):

            @pl.when(g != 1 + h)
            def _():
                early_out(h).wait_send()
                for c in range(4):
                    late_out(h, c).wait_send()

    @pl.when(adds)
    def _():
        for j in (1, 2, 3):
            early_sum_out(j).wait_send()

    for h in range(2):

        @pl.when(g != 1 + h)
        def _():
            early_sum_from(h).wait_recv()

    def away(c):
        return remote(stage.at[1 - k, c], back.at[c], bs.at[c], br.at[c], sib)

    for c in range(4):
        for h in range(2):

            @pl.when(g != 1 + h)
            def _():
                late_sum_from(h, c).wait_recv()

            stage[h, c] = (early_sum[h, c].astype(F32) + late_sum[h, c].astype(F32)).T
        away(c).start()
    for c in range(4):
        away(c).wait_recv()
        here = slice(c * PART, (c + 1) * PART)

        @pl.when(role == 0)
        def _():
            o_ref[here, :PART] = stage[k, c]
            o_ref[here, PART:] = back[c]

        @pl.when(role == 1)
        def _():
            o_ref[here, :PART] = back[c]
            o_ref[here, PART:] = stage[k, c]

    for c in range(4):
        away(c).wait_send()

    @pl.when(adds)
    def _():
        for j in (1, 2, 3):
            for c in range(4):
                late_sum_out(j, c).wait_send()


def pseudo_of(outer_params, first_moment, second_moment, activations, targets):
    dma = pltpu.SemaphoreType.DMA
    vm = pltpu.VMEM
    hbm = pl.BlockSpec(memory_space=pltpu.HBM)
    n = STEPS
    tile = (PART, PART)
    return pl.pallas_call(
        kernel,
        out_shape=jax.ShapeDtypeStruct((512, 256), F32),
        in_specs=[hbm] * 5,
        out_specs=pl.BlockSpec(memory_space=pltpu.VMEM),
        scratch_shapes=[
            vm((n, 4, 2, 512, 512), BF16),
            vm((3, 2, 512, PART), F32),
            vm((PART, 1024), F32), vm((PART, 1024), F32), vm((PART, 1024), F32), vm((PART, 1024), F32),
            vm((PART, 1024), BF16),
            vm((4, n, *tile), BF16),
            vm((4, *tile), F32),
            vm((n, 4, 4, *tile), BF16), vm((n, 4, 4, *tile), BF16),
            vm((4, *tile), F32),
            vm((n, 4, *tile), BF16), vm((n, 4, *tile), BF16),
            vm((n, 4, 4, *tile), BF16),
            vm((PART, 1024), F32),
            vm((2, 4, *tile), F32), vm((4, *tile), F32),
            vm((2, 4, *tile), BF16), vm((2, 4, *tile), BF16), vm((2, 4, *tile), BF16),
            vm((4, *tile), F32),
            vm((2, 4, *tile), BF16), vm((2, 4, *tile), BF16), vm((2, 4, *tile), BF16),
            vm((2, 4, *tile), F32), vm((4, *tile), F32),
            dma((7,)),
            dma((n, 6)), dma((n, 6)), dma((n, 8)), dma((n, 8)),
            dma((3,)), dma((3,)), dma((2,)), dma((4,)),
            dma((n, 4, 4)), dma((n, 4, 4)), dma((n, 4)), dma((n, 4)),
            dma((n, 4, 4)), dma((n, 4, 4)),
            dma((2,)), dma, dma((2,)), dma((2,)), dma((4,)), dma((2,)),
            dma((2, 4)), dma((2, 4)), dma((4, 4)), dma((2, 4)),
            dma((4,)), dma((4,)),
        ],
        compiler_params=pltpu.CompilerParams(
            collective_id=0, has_side_effects=True, vmem_limit_bytes=48 << 20
        ),
    )(*[pltpu.with_memory_space_constraint(a, pltpu.HBM) for a in (outer_params, first_moment, second_moment, activations, targets)])


def local(outer_params, first_moment, second_moment, outer_moment, activations, targets):
    pseudo = pseudo_of(outer_params, first_moment, second_moment, activations, targets)
    new_moment = momentum_coef * outer_moment + pseudo
    new_params = outer_params - outer_rate * (pseudo + momentum_coef * new_moment)
    return (new_params, new_moment)


def solution(mesh):
    placed = (
        P("col", "row"),
        P("grp", "col", "row"),
        P("grp", "col", "row"),
        P("col", "row"),
        P("grp", None, "row", "col"),
        P("grp", None, "col", "row"),
    )
    return jax.shard_map(
        local,
        mesh=mesh,
        in_specs=placed,
        out_specs=(P("col", "row"), P("col", "row")),
        check_vma=False,
    )
```
